256 devices in a mesh: gx: 64 (over x, z, core), gy: 4 (over y).
Axes of the slice: x: 4, y: 4, z: 8, core: 2. Of those that a mesh axis runs over, the one named last changes fastest.
Arguments:
- velocity: float32 [2048, 512, 256], P('gx', 'gy'), may hold values from -6 to 6
- threshold_table: float32 [16], replicated, may hold values from 0.05 to 1.5
- band_index: int32 [3, 7], replicated, may hold values from 0 to 15
Outputs:
- updated: float32 [2048, 512, 256], P('gx', 'gy')
The draws below stay inside these ranges and needn't reach their ends.
All inputs are finite; a program needn't handle non-finite values.
Results may differ from the reference program's by a relative error of at most 0.0003.
Values sent between devices are 32-bit elements; how exact they have to be, the bound alone decides.
A program may use at most 128 MiB of HBM per device.

```python
import math
import jax
import jax.numpy as jnp
from jax import lax

NZ = 256
LEVELS = 3
TABLE = 16
NX = 2048
NY = 512


def set_ends(array, key, smallest, top_value):
    index_at = [jax.random.randint(jax.random.fold_in(key, axis), (), 0, length) for axis, length in enumerate(array.shape)]
    longest = array.shape.index(max(array.shape))
    neighbour = index_at[:longest] + [(index_at[longest] + 1) % array.shape[longest]] + index_at[longest + 1:]
    return array.at[tuple(index_at)].set(smallest).at[tuple(neighbour)].set(top_value)


def levels(rng, shape, pieces, least, high):
    loudness = 1.0
    for dim, parts in pieces:
        steps = jax.random.uniform(jax.random.fold_in(jax.random.fold_in(rng, 6), dim), (parts,), jnp.float32, least / len(pieces), high / len(pieces))
        loudness = loudness * jnp.repeat(jnp.exp(steps), shape[dim] // parts).reshape((-1,) + (1,) * (len(shape) - 1 - dim))
    return loudness


def scatter_about(rng, dims, scale, reach, cuts=(), kind=jnp.bfloat16):
    entries = scale * jax.random.normal(rng, dims, jnp.float32)
    if cuts:
        entries = entries * levels(rng, dims, cuts, -0.22, 0.18)
    return jnp.clip(entries, -reach, reach).astype(kind)


def setup_inputs(seed: int = 0) -> dict:
    seeds = jax.random.split(jax.random.key(seed), 4)
    velocity = scatter_about(seeds[0], (NX, NY, NZ), 1.0, 6.0, ((0, 64), (1, 4)), jnp.float32)
    threshold_table = jnp.clip(jnp.exp(jax.random.uniform(seeds[1], (TABLE,), jnp.float32, math.log(0.05), math.log(1.5))), 0.05, 1.5)
    band_index = set_ends(jax.random.randint(seeds[2], (LEVELS, 7), 0, TABLE), jax.random.fold_in(seeds[2], 1), 0, TABLE - 1).astype(jnp.int32)
    return {"velocity": velocity, "threshold_table": threshold_table, "band_index": band_index}


filt_low = [0.23037781330885523, 0.7148465705525415, 0.6308807679295904, -0.02798376941698385,
            -0.18703481171888114, 0.030841381835986965, 0.032883011666982945, -0.010597401784997278]
filt_high = [((-1.0) ** j) * filt_low[7 - j] for j in range(8)]


def wrapped(field, dim, width):
    size = field.shape[dim]
    left = lax.slice_in_dim(field, size - width, size, 1, dim)
    right = lax.slice_in_dim(field, 0, width, 1, dim)
    return jnp.concatenate([left, field, right], axis=dim)


def analyse(extended, dim):
    count = extended.shape[dim] - 6
    low = 0.0
    high = 0.0
    for j in range(8):
        taken = lax.slice_in_dim(extended, j, j + count - 1, 2, dim)
        low = low + filt_low[j] * taken
        high = high + filt_high[j] * taken
    return low, high


def synthesise(low_ext, high_ext, dim):
    half = low_ext.shape[dim] - 4
    even = 0.0
    odd = 0.0
    for j in range(8):
        if j % 2 == 1:
            start = (3 - j) // 2 + 2
        else:
            start = (4 - j) // 2 + 2
        term = filt_low[j] * lax.slice_in_dim(low_ext, start, start + half, 1, dim) + filt_high[j] * lax.slice_in_dim(high_ext, start, start + half, 1, dim)
        if j % 2 == 1:
            even = even + term
        else:
            odd = odd + term
    joined = jnp.stack([even, odd], axis=dim + 1)
    shape = list(even.shape)
    shape[dim] = 2 * half
    return joined.reshape(shape)


def depth_and_bands(ybands):
    zlow, zhigh = analyse(wrapped(ybands, 4, 3), 4)
    stacked = jnp.stack([zlow, zhigh], axis=2)
    return stacked.reshape((8,) + zlow.shape[2:])


def depth_synth(bands):
    split = bands.reshape((2, 2, 2) + bands.shape[1:])
    return synthesise(wrapped(split[:, :, 0], 4, 2), wrapped(split[:, :, 1], 4, 2), 4)


def shrink(bands, table, indices):
    match = indices[:, None] == jnp.arange(table.shape[0], dtype=jnp.int32)[None, :]
    thresh = jnp.sum(jnp.where(match, table[None, :], 0.0), axis=1)
    thresh = thresh[:, None, None, None]
    return jnp.sign(bands) * jnp.maximum(jnp.abs(bands) - thresh, 0.0)


def reference(velocity, threshold_table, band_index):
    approx = velocity
    details = []
    for level in range(LEVELS):
        low, high = analyse(wrapped(approx, 0, 3), 0)
        stacked = jnp.stack([low, high])
        ylow, yhigh = analyse(wrapped(stacked, 2, 3), 2)
        bands = depth_and_bands(jnp.stack([ylow, yhigh], axis=1))
        details.append(shrink(bands[1:], threshold_table, band_index[level]))
        approx = bands[0]
    recon = approx
    for level in range(LEVELS - 1, -1, -1):
        bands = jnp.concatenate([recon[None], details[level]], axis=0)
        yzpart = depth_synth(bands)
        extended = wrapped(yzpart, 3, 2)
        ypart = synthesise(extended[:, 0], extended[:, 1], 2)
        extended = wrapped(ypart, 1, 2)
        recon = synthesise(extended[0], extended[1], 0)
    return recon
```

```python
import jax
import jax.numpy as jnp
import numpy as np
from jax import lax
from jax.sharding import PartitionSpec as P

LEVELS = 3
PREC = lax.Precision.HIGH

filt_low = [
    0.23037781330885523,
    0.7148465705525415,
    0.6308807679295904,
    -0.02798376941698385,
    -0.18703481171888114,
    0.030841381835986965,
    0.032883011666982945,
    -0.010597401784997278,
]
filt_high = [(-1.0) ** j * filt_low[7 - j] for j in range(8)]


def split_analysis(length):
    matrix = np.zeros((length + 6, length), np.float32)
    for k in range(length // 2):
        for j in range(8):
            matrix[2 * k + j, k] = filt_low[j]
            matrix[2 * k + j, length // 2 + k] = filt_high[j]
    return matrix


def periodic_analysis(length):
    matrix = np.zeros((length, length), np.float32)
    for k in range(length // 2):
        for j in range(8):
            matrix[(2 * k + j - 3) % length, k] += filt_low[j]
            matrix[(2 * k + j - 3) % length, length // 2 + k] += filt_high[j]
    return matrix


def split_synthesis(length):
    half_len = length // 2
    matrix = np.zeros((2, half_len + 4, length), np.float32)
    for position in range(half_len + 4):
        k = position - 2
        for m in range(length):
            j = m + 3 - 2 * k
            if 0 <= j < 8:
                matrix[0, position, m] = filt_low[j]
                matrix[1, position, m] = filt_high[j]
    return matrix.reshape(2 * (half_len + 4), length)


def shifted(block, axes, shifts):
    sizes = [lax.axis_size(axis) for axis in axes]
    if len(axes) == 1:
        size, shift = sizes[0], shifts[0]
        pairs = [(i, (i + shift) % size) for i in range(size)]
        return lax.ppermute(block, axes[0], pairs)
    size_x, size_y = sizes
    pairs = []
    for i in range(size_x):
        for j in range(size_y):
            dest = ((i + shifts[0]) % size_x) * size_y + (j + shifts[1]) % size_y
            pairs.append((i * size_y + j, dest))
    return lax.ppermute(block, tuple(axes), pairs)


def halo(array, dx, hx, dy, hy):
    size_x, size_y = array.shape[dx], array.shape[dy]
    cut = lax.slice_in_dim
    last_x = cut(array, size_x - hx, size_x, axis=dx)
    first_x = cut(array, 0, hx, axis=dx)
    before_x = shifted(last_x, ("gx",), (1,))
    after_x = shifted(first_x, ("gx",), (-1,))
    before_y = shifted(cut(array, size_y - hy, size_y, axis=dy), ("gy",), (1,))
    after_y = shifted(cut(array, 0, hy, axis=dy), ("gy",), (-1,))
    corner_bb = shifted(cut(last_x, size_y - hy, size_y, axis=dy), ("gx", "gy"), (1, 1))
    corner_ba = shifted(cut(last_x, 0, hy, axis=dy), ("gx", "gy"), (1, -1))
    corner_ab = shifted(cut(first_x, size_y - hy, size_y, axis=dy), ("gx", "gy"), (-1, 1))
    corner_aa = shifted(cut(first_x, 0, hy, axis=dy), ("gx", "gy"), (-1, -1))
    top = jnp.concatenate([corner_bb, before_x, corner_ba], axis=dy)
    mid = jnp.concatenate([before_y, array, after_y], axis=dy)
    bottom = jnp.concatenate([corner_ab, after_x, corner_aa], axis=dy)
    return jnp.concatenate([top, mid, bottom], axis=dx)


def contract(left, right, dims, batch):
    return lax.dot_general(
        left, right, (dims, batch), precision=PREC, preferred_element_type=jnp.float32
    )


def batched_left(matrix, data):
    spread = jnp.broadcast_to(jnp.asarray(matrix), (data.shape[0],) + matrix.shape)
    return contract(spread, data, ((1,), (1,)), ((0,), (0,)))


def analyse_lead(extended):
    count = extended.shape[0] - 6
    low = 0.0
    high = 0.0
    for j in range(8):
        taken = lax.slice_in_dim(extended, j, j + count - 1, 2, 0)
        low = low + filt_low[j] * taken
        high = high + filt_high[j] * taken
    return jnp.concatenate([low, high], axis=0)


def synthesise_lead(low_ext, high_ext):
    half = low_ext.shape[0] - 4
    even = 0.0
    odd = 0.0
    for j in range(8):
        if j % 2 == 1:
            start = (3 - j) // 2 + 2
        else:
            start = (4 - j) // 2 + 2
        term = filt_low[j] * low_ext[start : start + half] + filt_high[j] * high_ext[start : start + half]
        if j % 2 == 1:
            even = even + term
        else:
            odd = odd + term
    joined = jnp.stack([even, odd], axis=1)
    return joined.reshape((2 * half,) + even.shape[1:])


def analysis_level(approx):
    size_x, size_y, size_z = approx.shape
    extended = halo(approx, 0, 3, 1, 3)
    x_part = analyse_lead(extended)
    y_part = batched_left(split_analysis(size_y), x_part)
    return contract(y_part, jnp.asarray(periodic_analysis(size_z)), ((2,), (0,)), ((), ()))


def shrink_field(coeffs, thr_table, indices):
    size_x, size_y, size_z = coeffs.shape
    matched = indices[:, None] == jnp.arange(thr_table.shape[0], dtype=jnp.int32)[None, :]
    seven = jnp.sum(jnp.where(matched, thr_table[None, :], 0.0), axis=1)
    eight = jnp.concatenate([jnp.zeros((1,), jnp.float32), seven])
    high_x = (jnp.arange(size_x, dtype=jnp.int32) >= size_x // 2).astype(jnp.int32)
    high_y = (jnp.arange(size_y, dtype=jnp.int32) >= size_y // 2).astype(jnp.int32)
    high_z = (jnp.arange(size_z, dtype=jnp.int32) >= size_z // 2).astype(jnp.int32)
    band_ids = 4 * high_x[:, None, None] + 2 * high_y[None, :, None] + high_z[None, None, :]
    thresh = jnp.zeros(coeffs.shape, jnp.float32)
    for band_no in range(1, 8):
        thresh = jnp.where(band_ids == band_no, eight[band_no], thresh)
    return jnp.sign(coeffs) * jnp.maximum(jnp.abs(coeffs) - thresh, 0.0)


def synthesis_level(detail_ext, recon):
    two, hx4, _, hy4, size_z = detail_ext.shape
    recon_ext = halo(recon, 0, 2, 1, 2)
    full = detail_ext.at[0, :, 0, :, : size_z // 2].set(recon_ext)
    z_part = contract(full, jnp.asarray(periodic_analysis(size_z)), ((4,), (1,)), ((), ()))
    size_y = 2 * (hy4 - 4)
    y_in = z_part.reshape(2 * hx4, 2 * hy4, size_z)
    y_part = batched_left(split_synthesis(size_y), y_in).reshape(2, hx4, size_y, size_z)
    return synthesise_lead(y_part[0], y_part[1])


def local(velocity, threshold_table, band_index):
    approx = velocity
    detail_list = []
    for level_no in range(LEVELS):
        coeffs = analysis_level(approx)
        shrunk = shrink_field(coeffs, threshold_table, band_index[level_no])
        size_x, size_y, size_z = coeffs.shape
        blocked = shrunk.reshape(2, size_x // 2, 2, size_y // 2, size_z)
        detail_list.append(halo(blocked, 1, 2, 3, 2))
        approx = coeffs[: size_x // 2, : size_y // 2, : size_z // 2]
    rebuilt = approx
    for level_no in range(LEVELS - 1, -1, -1):
        rebuilt = synthesis_level(detail_list[level_no], rebuilt)
    return rebuilt


def solution(mesh):
    return jax.shard_map(
        local,
        mesh=mesh,
        in_specs=(P("gx", "gy", None), P(), P()),
        out_specs=P("gx", "gy", None),
        check_vma=False,
    )
```

```python
import functools

import jax
import jax.numpy as jnp
import numpy as np
from jax import lax
from jax.experimental import pallas as pl
from jax.experimental.pallas import tpu as pltpu
from jax.sharding import PartitionSpec as P

LEVELS = 3
PREC = lax.Precision.HIGH

filt_low = [
    0.23037781330885523,
    0.7148465705525415,
    0.6308807679295904,
    -0.02798376941698385,
    -0.18703481171888114,
    0.030841381835986965,
    0.032883011666982945,
    -0.010597401784997278,
]
filt_high = [(-1.0) ** j * filt_low[7 - j] for j in range(8)]


def split_analysis(length):
    matrix = np.zeros((length + 6, length), np.float32)
    for k in range(length // 2):
        for j in range(8):
            matrix[2 * k + j, k] = filt_low[j]
            matrix[2 * k + j, length // 2 + k] = filt_high[j]
    return matrix


def periodic_analysis(length):
    matrix = np.zeros((length, length), np.float32)
    for k in range(length // 2):
        for j in range(8):
            matrix[(2 * k + j - 3) % length, k] += filt_low[j]
            matrix[(2 * k + j - 3) % length, length // 2 + k] += filt_high[j]
    return matrix


def split_synthesis(length):
    half_len = length // 2
    matrix = np.zeros((2, half_len + 4, length), np.float32)
    for position in range(half_len + 4):
        k = position - 2
        for m in range(length):
            j = m + 3 - 2 * k
            if 0 <= j < 8:
                matrix[0, position, m] = filt_low[j]
                matrix[1, position, m] = filt_high[j]
    return matrix


OFFSETS = ((1, 0), (-1, 0), (0, 1), (0, -1), (1, 1), (1, -1), (-1, 1), (-1, -1))
EXCHANGE_IDS = [0]


def exchange_kernel(size_x, size_y, *refs):
    count = len(OFFSETS)
    sources, targets = refs[:count], refs[count : 2 * count]
    send_sem, recv_sem = refs[2 * count], refs[2 * count + 1]
    me_x = lax.axis_index("gx")
    me_y = lax.axis_index("gy")
    peers = [
        (lax.rem(me_x + np.int32(dx + size_x), np.int32(size_x)), lax.rem(me_y + np.int32(dy + size_y), np.int32(size_y)))
        for dx, dy in OFFSETS
    ]
    barrier = pltpu.get_barrier_semaphore()
    for peer in peers:
        pl.semaphore_signal(barrier, inc=1, device_id=peer, device_id_type=pl.DeviceIdType.MESH)
    pl.semaphore_wait(barrier, count)
    copies = []
    for slot, peer in enumerate(peers):
        copy = pltpu.make_async_remote_copy(
            src_ref=sources[slot],
            dst_ref=targets[slot],
            send_sem=send_sem.at[slot],
            recv_sem=recv_sem.at[slot],
            device_id=peer,
            device_id_type=pl.DeviceIdType.MESH,
        )
        copy.start()
        copies.append(copy)
    for copy in copies:
        copy.wait()


def exchange(pieces):
    cid = EXCHANGE_IDS[0]
    EXCHANGE_IDS[0] += 1
    count = len(OFFSETS)
    return pl.pallas_call(
        functools.partial(exchange_kernel, lax.axis_size("gx"), lax.axis_size("gy")),
        out_shape=[jax.ShapeDtypeStruct(p.shape, p.dtype) for p in pieces],
        in_specs=[pl.BlockSpec(memory_space=pl.ANY)] * count,
        out_specs=[pl.BlockSpec(memory_space=pl.ANY)] * count,
        scratch_shapes=[pltpu.SemaphoreType.DMA((count,)), pltpu.SemaphoreType.DMA((count,))],
        compiler_params=pltpu.CompilerParams(collective_id=cid, has_side_effects=True),
    )(*pieces)


def halo(array, dx, hx, dy, hy):
    size_x, size_y = array.shape[dx], array.shape[dy]
    cut = lax.slice_in_dim
    last_x = cut(array, size_x - hx, size_x, axis=dx)
    first_x = cut(array, 0, hx, axis=dx)
    pieces = [
        last_x,
        first_x,
        cut(array, size_y - hy, size_y, axis=dy),
        cut(array, 0, hy, axis=dy),
        cut(last_x, size_y - hy, size_y, axis=dy),
        cut(last_x, 0, hy, axis=dy),
        cut(first_x, size_y - hy, size_y, axis=dy),
        cut(first_x, 0, hy, axis=dy),
    ]
    before_x, after_x, before_y, after_y, corner_bb, corner_ba, corner_ab, corner_aa = exchange(pieces)
    top = jnp.concatenate([corner_bb, before_x, corner_ba], axis=dy)
    mid = jnp.concatenate([before_y, array, after_y], axis=dy)
    bottom = jnp.concatenate([corner_ab, after_x, corner_aa], axis=dy)
    return jnp.concatenate([top, mid, bottom], axis=dx)


def contract(left, right, dims, batch):
    return lax.dot_general(
        left, right, (dims, batch), precision=PREC, preferred_element_type=jnp.float32
    )


def batched_left(matrix, data):
    spread = jnp.broadcast_to(jnp.asarray(matrix), (data.shape[0],) + matrix.shape)
    return contract(spread, data, ((1,), (1,)), ((0,), (0,)))


def analyse_lead(extended):
    count = extended.shape[0] - 6
    low = 0.0
    high = 0.0
    for j in range(8):
        taken = lax.slice_in_dim(extended, j, j + count - 1, 2, 0)
        low = low + filt_low[j] * taken
        high = high + filt_high[j] * taken
    return jnp.concatenate([low, high], axis=0)


def synthesise_lead(low_ext, high_ext):
    half = low_ext.shape[0] - 4
    even = 0.0
    odd = 0.0
    for j in range(8):
        if j % 2 == 1:
            start = (3 - j) // 2 + 2
        else:
            start = (4 - j) // 2 + 2
        term = filt_low[j] * low_ext[start : start + half] + filt_high[j] * high_ext[start : start + half]
        if j % 2 == 1:
            even = even + term
        else:
            odd = odd + term
    joined = jnp.stack([even, odd], axis=1)
    return joined.reshape((2 * half,) + even.shape[1:])


def analysis_level(approx):
    size_x, size_y, size_z = approx.shape
    extended = halo(approx, 0, 3, 1, 3)
    x_part = analyse_lead(extended)
    y_part = batched_left(split_analysis(size_y), x_part)
    return contract(y_part, jnp.asarray(periodic_analysis(size_z)), ((2,), (0,)), ((), ()))


def shrink_field(coeffs, thr_table, indices):
    size_x, size_y, size_z = coeffs.shape
    matched = indices[:, None] == jnp.arange(thr_table.shape[0], dtype=jnp.int32)[None, :]
    seven = jnp.sum(jnp.where(matched, thr_table[None, :], 0.0), axis=1)
    eight = jnp.concatenate([jnp.zeros((1,), jnp.float32), seven])
    high_x = (jnp.arange(size_x, dtype=jnp.int32) >= size_x // 2).astype(jnp.int32)
    high_y = (jnp.arange(size_y, dtype=jnp.int32) >= size_y // 2).astype(jnp.int32)
    high_z = (jnp.arange(size_z, dtype=jnp.int32) >= size_z // 2).astype(jnp.int32)
    band_ids = 4 * high_x[:, None, None] + 2 * high_y[None, :, None] + high_z[None, None, :]
    thresh = jnp.zeros(coeffs.shape, jnp.float32)
    for band_no in range(1, 8):
        thresh = jnp.where(band_ids == band_no, eight[band_no], thresh)
    return jnp.sign(coeffs) * jnp.maximum(jnp.abs(coeffs) - thresh, 0.0)


def synthesis_level(shrunk, recon):
    size_x, size_y, size_z = shrunk.shape
    full = lax.dynamic_update_slice(shrunk, recon, (0, 0, 0))
    blocked = full.reshape(2, size_x // 2, 2, size_y // 2, size_z)
    extended = halo(blocked, 1, 2, 3, 2)
    hx4 = size_x // 2 + 4
    z_part = contract(extended, jnp.asarray(periodic_analysis(size_z)), ((4,), (1,)), ((), ()))
    z_part = z_part.reshape(2 * hx4, 2, size_y // 2 + 4, size_z)
    matrix = split_synthesis(size_y)
    y_part = batched_left(matrix[0], z_part[:, 0]) + batched_left(matrix[1], z_part[:, 1])
    y_part = y_part.reshape(2, hx4, size_y, size_z)
    return synthesise_lead(y_part[0], y_part[1])


def local(velocity, threshold_table, band_index):
    EXCHANGE_IDS[0] = 0
    approx = velocity
    detail_list = []
    for level_no in range(LEVELS):
        coeffs = analysis_level(approx)
        detail_list.append(shrink_field(coeffs, threshold_table, band_index[level_no]))
        size_x, size_y, size_z = coeffs.shape
        approx = coeffs[: size_x // 2, : size_y // 2, : size_z // 2]
    rebuilt = approx
    for level_no in range(LEVELS - 1, -1, -1):
        rebuilt = synthesis_level(detail_list[level_no], rebuilt)
    return rebuilt


def solution(mesh):
    return jax.shard_map(
        local,
        mesh=mesh,
        in_specs=(P("gx", "gy", None), P(), P()),
        out_specs=P("gx", "gy", None),
        check_vma=False,
    )
```

```python
import functools

import jax
import jax.numpy as jnp
import numpy as np
from jax import lax
from jax.experimental import pallas as pl
from jax.experimental.pallas import tpu as pltpu
from jax.sharding import PartitionSpec as P

LEVELS = 3
PREC = lax.Precision.HIGH

filt_low = [
    0.23037781330885523,
    0.7148465705525415,
    0.6308807679295904,
    -0.02798376941698385,
    -0.18703481171888114,
    0.030841381835986965,
    0.032883011666982945,
    -0.010597401784997278,
]
filt_high = [(-1.0) ** j * filt_low[7 - j] for j in range(8)]


def split_analysis(length):
    matrix = np.zeros((length + 6, length), np.float32)
    for k in range(length // 2):
        for j in range(8):
            matrix[2 * k + j, k] = filt_low[j]
            matrix[2 * k + j, length // 2 + k] = filt_high[j]
    return matrix


def periodic_analysis(length):
    matrix = np.zeros((length, length), np.float32)
    for k in range(length // 2):
        for j in range(8):
            matrix[(2 * k + j - 3) % length, k] += filt_low[j]
            matrix[(2 * k + j - 3) % length, length // 2 + k] += filt_high[j]
    return matrix


def split_synthesis(length):
    half_len = length // 2
    matrix = np.zeros((2, half_len + 4, length), np.float32)
    for position in range(half_len + 4):
        k = position - 2
        for m in range(length):
            j = m + 3 - 2 * k
            if 0 <= j < 8:
                matrix[0, position, m] = filt_low[j]
                matrix[1, position, m] = filt_high[j]
    return matrix


OFFSETS = ((1, 0), (-1, 0), (0, 1), (0, -1), (1, 1), (1, -1), (-1, 1), (-1, -1))
EXCHANGE_IDS = [0]


def exchange_kernel(size_x, size_y, *refs):
    count = len(OFFSETS)
    sources, targets = refs[:count], refs[count : 2 * count]
    send_sem, recv_sem = refs[2 * count], refs[2 * count + 1]
    me_x = lax.axis_index("gx")
    me_y = lax.axis_index("gy")
    peers = [
        (lax.rem(me_x + np.int32(dx + size_x), np.int32(size_x)), lax.rem(me_y + np.int32(dy + size_y), np.int32(size_y)))
        for dx, dy in OFFSETS
    ]
    barrier = pltpu.get_barrier_semaphore()
    for peer in peers:
        pl.semaphore_signal(barrier, inc=1, device_id=peer, device_id_type=pl.DeviceIdType.MESH)
    pl.semaphore_wait(barrier, count)
    copies = []
    for slot, peer in enumerate(peers):
        copy = pltpu.make_async_remote_copy(
            src_ref=sources[slot],
            dst_ref=targets[slot],
            send_sem=send_sem.at[slot],
            recv_sem=recv_sem.at[slot],
            device_id=peer,
            device_id_type=pl.DeviceIdType.MESH,
        )
        copy.start()
        copies.append(copy)
    for copy in copies:
        copy.wait()


def exchange(pieces):
    cid = EXCHANGE_IDS[0]
    EXCHANGE_IDS[0] += 1
    count = len(OFFSETS)
    return pl.pallas_call(
        functools.partial(exchange_kernel, lax.axis_size("gx"), lax.axis_size("gy")),
        out_shape=[jax.ShapeDtypeStruct(p.shape, p.dtype) for p in pieces],
        in_specs=[pl.BlockSpec(memory_space=pl.ANY)] * count,
        out_specs=[pl.BlockSpec(memory_space=pl.ANY)] * count,
        scratch_shapes=[pltpu.SemaphoreType.DMA((count,)), pltpu.SemaphoreType.DMA((count,))],
        compiler_params=pltpu.CompilerParams(collective_id=cid, has_side_effects=True),
    )(*pieces)


def halo(array, dx, hx, dy, hy):
    size_x, size_y = array.shape[dx], array.shape[dy]
    cut = lax.slice_in_dim
    last_x = cut(array, size_x - hx, size_x, axis=dx)
    first_x = cut(array, 0, hx, axis=dx)
    pieces = [
        last_x,
        first_x,
        cut(array, size_y - hy, size_y, axis=dy),
        cut(array, 0, hy, axis=dy),
        cut(last_x, size_y - hy, size_y, axis=dy),
        cut(last_x, 0, hy, axis=dy),
        cut(first_x, size_y - hy, size_y, axis=dy),
        cut(first_x, 0, hy, axis=dy),
    ]
    before_x, after_x, before_y, after_y, corner_bb, corner_ba, corner_ab, corner_aa = exchange(pieces)
    top = jnp.concatenate([corner_bb, before_x, corner_ba], axis=dy)
    mid = jnp.concatenate([before_y, array, after_y], axis=dy)
    bottom = jnp.concatenate([corner_ab, after_x, corner_aa], axis=dy)
    return jnp.concatenate([top, mid, bottom], axis=dx)


def contract(left, right, dims, batch):
    return lax.dot_general(
        left, right, (dims, batch), precision=PREC, preferred_element_type=jnp.float32
    )


def batched_left(matrix, data):
    spread = jnp.broadcast_to(jnp.asarray(matrix), (data.shape[0],) + matrix.shape)
    return contract(spread, data, ((1,), (1,)), ((0,), (0,)))


def analyse_lead(extended):
    count = extended.shape[0] - 6
    low = 0.0
    high = 0.0
    for j in range(8):
        taken = lax.slice_in_dim(extended, j, j + count - 1, 2, 0)
        low = low + filt_low[j] * taken
        high = high + filt_high[j] * taken
    return jnp.concatenate([low, high], axis=0)


def synthesise_lead(low_ext, high_ext):
    half = low_ext.shape[0] - 4
    even = 0.0
    odd = 0.0
    for j in range(8):
        if j % 2 == 1:
            start = (3 - j) // 2 + 2
        else:
            start = (4 - j) // 2 + 2
        term = filt_low[j] * low_ext[start : start + half] + filt_high[j] * high_ext[start : start + half]
        if j % 2 == 1:
            even = even + term
        else:
            odd = odd + term
    joined = jnp.stack([even, odd], axis=1)
    return joined.reshape((2 * half,) + even.shape[1:])


def analysis_ext(extended):
    x_part = analyse_lead(extended)
    y_part = batched_left(split_analysis(x_part.shape[1] - 6), x_part)
    size_z = y_part.shape[2]
    return contract(y_part, jnp.asarray(periodic_analysis(size_z)), ((2,), (0,)), ((), ()))


def shrink_field(coeffs, thr_table, indices):
    size_x, size_y, size_z = coeffs.shape
    matched = indices[:, None] == jnp.arange(thr_table.shape[0], dtype=jnp.int32)[None, :]
    seven = jnp.sum(jnp.where(matched, thr_table[None, :], 0.0), axis=1)
    eight = jnp.concatenate([jnp.zeros((1,), jnp.float32), seven])
    high_x = (jnp.arange(size_x, dtype=jnp.int32) >= size_x // 2).astype(jnp.int32)
    high_y = (jnp.arange(size_y, dtype=jnp.int32) >= size_y // 2).astype(jnp.int32)
    high_z = (jnp.arange(size_z, dtype=jnp.int32) >= size_z // 2).astype(jnp.int32)
    band_ids = 4 * high_x[:, None, None] + 2 * high_y[None, :, None] + high_z[None, None, :]
    thresh = jnp.zeros(coeffs.shape, jnp.float32)
    for band_no in range(1, 8):
        thresh = jnp.where(band_ids == band_no, eight[band_no], thresh)
    return jnp.sign(coeffs) * jnp.maximum(jnp.abs(coeffs) - thresh, 0.0)


def synthesis_ext(extended):
    two, hx4, _, hy4, size_z = extended.shape
    z_part = contract(extended, jnp.asarray(periodic_analysis(size_z)), ((4,), (1,)), ((), ()))
    z_part = z_part.reshape(2 * hx4, 2, hy4, size_z)
    size_y = 2 * (hy4 - 4)
    matrix = split_synthesis(size_y)
    y_part = batched_left(matrix[0], z_part[:, 0]) + batched_left(matrix[1], z_part[:, 1])
    y_part = y_part.reshape(2, hx4, size_y, size_z)
    return synthesise_lead(y_part[0], y_part[1])


def blocked(cube):
    size_x, size_y, size_z = cube.shape
    return cube.reshape(2, size_x // 2, 2, size_y // 2, size_z)


def low_corner(cube):
    size_x, size_y, size_z = cube.shape
    return cube[: size_x // 2, : size_y // 2, : size_z // 2]


def local(velocity, threshold_table, band_index):
    EXCHANGE_IDS[0] = 0
    cube0 = analysis_ext(halo(velocity, 0, 3, 1, 3))
    shrunk0 = shrink_field(cube0, threshold_table, band_index[0])
    cube1 = analysis_ext(halo(low_corner(cube0), 0, 9, 1, 9))
    shrunk1 = blocked(shrink_field(cube1, threshold_table, band_index[1]))
    cube2 = analysis_ext(low_corner(cube1))
    shrunk2 = shrink_field(cube2, threshold_table, band_index[2])
    full2 = lax.dynamic_update_slice(shrunk2, low_corner(cube2), (0, 0, 0))
    recon2 = synthesis_ext(halo(blocked(full2), 1, 3, 3, 3))
    hx, hy = shrunk1.shape[1], shrunk1.shape[3]
    full1 = shrunk1[:, 1 : hx - 1, :, 1 : hy - 1, :]
    half_z = full1.shape[4] // 2
    full1 = full1.at[0, :, 0, :, :half_z].set(recon2)
    recon1 = synthesis_ext(full1)
    full0 = lax.dynamic_update_slice(shrunk0, recon1, (0, 0, 0))
    return synthesis_ext(halo(blocked(full0), 1, 2, 3, 2))


def solution(mesh):
    return jax.shard_map(
        local,
        mesh=mesh,
        in_specs=(P("gx", "gy", None), P(), P()),
        out_specs=P("gx", "gy", None),
        check_vma=False,
    )
```

```python
import functools

import jax
import jax.numpy as jnp
import numpy as np
from jax import lax
from jax.experimental import pallas as pl
from jax.experimental.pallas import tpu as pltpu
from jax.sharding import PartitionSpec as P

LEVELS = 3
PREC = lax.Precision.HIGH

filt_low = [
    0.23037781330885523,
    0.7148465705525415,
    0.6308807679295904,
    -0.02798376941698385,
    -0.18703481171888114,
    0.030841381835986965,
    0.032883011666982945,
    -0.010597401784997278,
]
filt_high = [(-1.0) ** j * filt_low[7 - j] for j in range(8)]


def split_analysis(length):
    matrix = np.zeros((length + 6, length), np.float32)
    for k in range(length // 2):
        for j in range(8):
            matrix[2 * k + j, k] = filt_low[j]
            matrix[2 * k + j, length // 2 + k] = filt_high[j]
    return matrix


def periodic_analysis(length):
    matrix = np.zeros((length, length), np.float32)
    for k in range(length // 2):
        for j in range(8):
            matrix[(2 * k + j - 3) % length, k] += filt_low[j]
            matrix[(2 * k + j - 3) % length, length // 2 + k] += filt_high[j]
    return matrix


def split_synthesis(length):
    half_len = length // 2
    matrix = np.zeros((2, half_len + 4, length), np.float32)
    for position in range(half_len + 4):
        k = position - 2
        for m in range(length):
            j = m + 3 - 2 * k
            if 0 <= j < 8:
                matrix[0, position, m] = filt_low[j]
                matrix[1, position, m] = filt_high[j]
    return matrix


OFFSETS = ((1, 0), (-1, 0), (0, 1), (0, -1), (1, 1), (1, -1), (-1, 1), (-1, -1))
EXCHANGE_IDS = [0]


def spans(offset, halo_len, size):
    if offset == 1:
        return halo_len + size - halo_len, 0, halo_len
    if offset == -1:
        return halo_len, halo_len + size, halo_len
    return halo_len, halo_len, size


def fill_kernel(layout, in_ref, out_ref, send_sem, recv_sem):
    ndim, dim_x, dim_y, hx, hy, size_x, size_y, mesh_x, mesh_y = layout
    me_x = lax.axis_index("gx")
    me_y = lax.axis_index("gy")
    peers = [
        (lax.rem(me_x + np.int32(ox + mesh_x), np.int32(mesh_x)), lax.rem(me_y + np.int32(oy + mesh_y), np.int32(mesh_y)))
        for ox, oy in OFFSETS
    ]
    barrier = pltpu.get_barrier_semaphore()
    for peer in peers:
        pl.semaphore_signal(barrier, inc=1, device_id=peer, device_id_type=pl.DeviceIdType.MESH)
    pl.semaphore_wait(barrier, len(OFFSETS))
    copies = []
    for slot, ((ox, oy), peer) in enumerate(zip(OFFSETS, peers)):
        source = [slice(None)] * ndim
        target = [slice(None)] * ndim
        sx, tx, lx = spans(ox, hx, size_x)
        sy, ty, ly = spans(oy, hy, size_y)
        source[dim_x], target[dim_x] = pl.ds(sx, lx), pl.ds(tx, lx)
        source[dim_y], target[dim_y] = pl.ds(sy, ly), pl.ds(ty, ly)
        copy = pltpu.make_async_remote_copy(
            src_ref=in_ref.at[tuple(source)],
            dst_ref=out_ref.at[tuple(target)],
            send_sem=send_sem.at[slot],
            recv_sem=recv_sem.at[slot],
            device_id=peer,
            device_id_type=pl.DeviceIdType.MESH,
        )
        copy.start()
        copies.append(copy)
    for copy in copies:
        copy.wait()


def fill_halo(padded, dim_x, hx, dim_y, hy):
    cid = EXCHANGE_IDS[0]
    EXCHANGE_IDS[0] += 1
    count = len(OFFSETS)
    size_x = padded.shape[dim_x] - 2 * hx
    size_y = padded.shape[dim_y] - 2 * hy
    layout = (padded.ndim, dim_x, dim_y, hx, hy, size_x, size_y, lax.axis_size("gx"), lax.axis_size("gy"))
    return pl.pallas_call(
        functools.partial(fill_kernel, layout),
        out_shape=jax.ShapeDtypeStruct(padded.shape, padded.dtype),
        in_specs=[pl.BlockSpec(memory_space=pl.ANY)],
        out_specs=pl.BlockSpec(memory_space=pl.ANY),
        scratch_shapes=[pltpu.SemaphoreType.DMA((count,)), pltpu.SemaphoreType.DMA((count,))],
        input_output_aliases={0: 0},
        compiler_params=pltpu.CompilerParams(collective_id=cid, has_side_effects=True),
    )(padded)


def pad_dims(array, dim_x, hx, dim_y, hy):
    widths = [(0, 0)] * array.ndim
    widths[dim_x] = (hx, hx)
    widths[dim_y] = (hy, hy)
    return jnp.pad(array, widths)


def analysis_matrix(size, pad, out_halo):
    half = size // 2 + 2 * out_halo
    matrix = np.zeros((size + 2 * pad, 2 * half), np.float32)
    for col in range(half):
        k = col - out_halo
        for j in range(8):
            matrix[2 * k + j - 3 + pad, col] = filt_low[j]
            matrix[2 * k + j - 3 + pad, half + col] = filt_high[j]
    return matrix


def synthesis_matrix(size, pad, out_halo):
    matrix = np.zeros((2, size // 2 + 2 * pad, size + 2 * out_halo), np.float32)
    for row in range(size // 2 + 2 * pad):
        k = row - pad
        for col in range(size + 2 * out_halo):
            j = col - out_halo + 3 - 2 * k
            if 0 <= j < 8:
                matrix[0, row, col] = filt_low[j]
                matrix[1, row, col] = filt_high[j]
    return matrix


def contract(left, right, dims, batch):
    return lax.dot_general(
        left, right, (dims, batch), precision=PREC, preferred_element_type=jnp.float32
    )


def batched_left(matrix, data):
    spread = jnp.broadcast_to(jnp.asarray(matrix), (data.shape[0],) + matrix.shape)
    return contract(spread, data, ((1,), (1,)), ((0,), (0,)))


def analyse_lead(extended):
    count = extended.shape[0] - 6
    low = 0.0
    high = 0.0
    for j in range(8):
        taken = lax.slice_in_dim(extended, j, j + count - 1, 2, 0)
        low = low + filt_low[j] * taken
        high = high + filt_high[j] * taken
    return jnp.concatenate([low, high], axis=0)


def synthesise_lead(low_ext, high_ext):
    half = low_ext.shape[0] - 4
    even = 0.0
    odd = 0.0
    for j in range(8):
        if j % 2 == 1:
            start = (3 - j) // 2 + 2
        else:
            start = (4 - j) // 2 + 2
        term = filt_low[j] * low_ext[start : start + half] + filt_high[j] * high_ext[start : start + half]
        if j % 2 == 1:
            even = even + term
        else:
            odd = odd + term
    joined = jnp.stack([even, odd], axis=1)
    return joined.reshape((2 * half,) + even.shape[1:])


def analysis_ext(extended, size_y, pad_y, out_halo):
    x_part = analyse_lead(extended)
    y_part = batched_left(analysis_matrix(size_y, pad_y, out_halo), x_part)
    size_z = y_part.shape[2]
    return contract(y_part, jnp.asarray(periodic_analysis(size_z)), ((2,), (0,)), ((), ()))


def shrink_field(coeffs, thr_table, indices):
    size_x, size_y, size_z = coeffs.shape
    matched = indices[:, None] == jnp.arange(thr_table.shape[0], dtype=jnp.int32)[None, :]
    seven = jnp.sum(jnp.where(matched, thr_table[None, :], 0.0), axis=1)
    eight = jnp.concatenate([jnp.zeros((1,), jnp.float32), seven])
    high_x = (jnp.arange(size_x, dtype=jnp.int32) >= size_x // 2).astype(jnp.int32)
    high_y = (jnp.arange(size_y, dtype=jnp.int32) >= size_y // 2).astype(jnp.int32)
    high_z = (jnp.arange(size_z, dtype=jnp.int32) >= size_z // 2).astype(jnp.int32)
    band_ids = 4 * high_x[:, None, None] + 2 * high_y[None, :, None] + high_z[None, None, :]
    thresh = jnp.zeros(coeffs.shape, jnp.float32)
    for band_no in range(1, 8):
        thresh = jnp.where(band_ids == band_no, eight[band_no], thresh)
    return jnp.sign(coeffs) * jnp.maximum(jnp.abs(coeffs) - thresh, 0.0)


def synthesis_ext(extended, size_y, pad_y, out_halo):
    two, hx4, _, hy4, size_z = extended.shape
    z_part = contract(extended, jnp.asarray(periodic_analysis(size_z)), ((4,), (1,)), ((), ()))
    z_part = z_part.reshape(2 * hx4, 2, hy4, size_z)
    matrix = synthesis_matrix(size_y, pad_y, out_halo)
    y_part = batched_left(matrix[0], z_part[:, 0]) + batched_left(matrix[1], z_part[:, 1])
    y_part = y_part.reshape(2, hx4, matrix.shape[2], size_z)
    return synthesise_lead(y_part[0], y_part[1])


def blocked(cube):
    size_x, size_y, size_z = cube.shape
    return cube.reshape(2, size_x // 2, 2, size_y // 2, size_z)


def low_corner(cube):
    size_x, size_y, size_z = cube.shape
    return cube[: size_x // 2, : size_y // 2, : size_z // 2]


def local(velocity, threshold_table, band_index):
    EXCHANGE_IDS[0] = 0
    size_x, size_y, size_z = velocity.shape
    ext0 = fill_halo(pad_dims(velocity, 0, 3, 1, 8), 0, 3, 1, 8)
    cube0 = analysis_ext(ext0, size_y, 8, 0)
    shrunk0 = shrink_field(cube0, threshold_table, band_index[0])
    ext1 = fill_halo(pad_dims(low_corner(cube0), 0, 9, 1, 16), 0, 9, 1, 16)
    cube1 = analysis_ext(ext1, size_y // 2, 16, 3)
    shrunk1 = blocked(shrink_field(cube1, threshold_table, band_index[1]))
    cube2 = analysis_ext(low_corner(cube1), size_y // 4, 3, 0)
    shrunk2 = shrink_field(cube2, threshold_table, band_index[2])
    full2 = lax.dynamic_update_slice(shrunk2, low_corner(cube2), (0, 0, 0))
    ext2 = fill_halo(pad_dims(blocked(full2), 1, 3, 3, 8), 1, 3, 3, 8)
    recon2 = synthesis_ext(ext2, size_y // 4, 8, 3)
    full1 = shrunk1[:, 1 : shrunk1.shape[1] - 1]
    full1 = full1.at[0, :, 0, :, : full1.shape[4] // 2].set(recon2)
    recon1 = synthesis_ext(full1, size_y // 2, 3, 0)
    padded0 = pad_dims(blocked(shrunk0), 1, 2, 3, 8)
    padded0 = padded0.at[0, 2 : 2 + size_x // 2, 0, 8 : 8 + size_y // 2, : size_z // 2].set(recon1)
    ext0 = fill_halo(padded0, 1, 2, 3, 8)
    return synthesis_ext(ext0, size_y, 8, 0)


def solution(mesh):
    return jax.shard_map(
        local,
        mesh=mesh,
        in_specs=(P("gx", "gy", None), P(), P()),
        out_specs=P("gx", "gy", None),
        check_vma=False,
    )
```

```python
import functools

import jax
import jax.numpy as jnp
import numpy as np
from jax import lax
from jax.experimental import pallas as pl
from jax.experimental.pallas import tpu as pltpu
from jax.sharding import PartitionSpec as P

LEVELS = 3
PREC = lax.Precision.HIGH

filt_low = [
    0.23037781330885523,
    0.7148465705525415,
    0.6308807679295904,
    -0.02798376941698385,
    -0.18703481171888114,
    0.030841381835986965,
    0.032883011666982945,
    -0.010597401784997278,
]
filt_high = [(-1.0) ** j * filt_low[7 - j] for j in range(8)]


def split_analysis(length):
    matrix = np.zeros((length + 6, length), np.float32)
    for k in range(length // 2):
        for j in range(8):
            matrix[2 * k + j, k] = filt_low[j]
            matrix[2 * k + j, length // 2 + k] = filt_high[j]
    return matrix


def periodic_analysis(length):
    matrix = np.zeros((length, length), np.float32)
    for k in range(length // 2):
        for j in range(8):
            matrix[(2 * k + j - 3) % length, k] += filt_low[j]
            matrix[(2 * k + j - 3) % length, length // 2 + k] += filt_high[j]
    return matrix


def split_synthesis(length):
    half_len = length // 2
    matrix = np.zeros((2, half_len + 4, length), np.float32)
    for position in range(half_len + 4):
        k = position - 2
        for m in range(length):
            j = m + 3 - 2 * k
            if 0 <= j < 8:
                matrix[0, position, m] = filt_low[j]
                matrix[1, position, m] = filt_high[j]
    return matrix


OFFSETS = ((1, 0), (-1, 0), (0, 1), (0, -1), (1, 1), (1, -1), (-1, 1), (-1, -1))
EXCHANGE_IDS = [0]


def exchange_kernel(size_x, size_y, *refs):
    count = len(OFFSETS)
    total = (len(refs) - 2) // 2
    sources, targets = refs[:total], refs[total : 2 * total]
    send_sem, recv_sem = refs[2 * total], refs[2 * total + 1]
    me_x = lax.axis_index("gx")
    me_y = lax.axis_index("gy")
    peers = [
        (lax.rem(me_x + np.int32(dx + size_x), np.int32(size_x)), lax.rem(me_y + np.int32(dy + size_y), np.int32(size_y)))
        for dx, dy in OFFSETS
    ]
    barrier = pltpu.get_barrier_semaphore()
    for peer in peers:
        pl.semaphore_signal(barrier, inc=1, device_id=peer, device_id_type=pl.DeviceIdType.MESH)
    pl.semaphore_wait(barrier, count)
    copies = []
    for slot in range(len(sources)):
        peer = peers[slot % count]
        copy = pltpu.make_async_remote_copy(
            src_ref=sources[slot],
            dst_ref=targets[slot],
            send_sem=send_sem.at[slot],
            recv_sem=recv_sem.at[slot],
            device_id=peer,
            device_id_type=pl.DeviceIdType.MESH,
        )
        copy.start()
        copies.append(copy)
    for copy in copies:
        copy.wait()


def exchange(pieces):
    cid = EXCHANGE_IDS[0]
    EXCHANGE_IDS[0] += 1
    count = len(pieces)
    return pl.pallas_call(
        functools.partial(exchange_kernel, lax.axis_size("gx"), lax.axis_size("gy")),
        out_shape=[jax.ShapeDtypeStruct(p.shape, p.dtype) for p in pieces],
        in_specs=[pl.BlockSpec(memory_space=pl.ANY)] * count,
        out_specs=[pl.BlockSpec(memory_space=pl.ANY)] * count,
        scratch_shapes=[pltpu.SemaphoreType.DMA((count,)), pltpu.SemaphoreType.DMA((count,))],
        compiler_params=pltpu.CompilerParams(collective_id=cid, has_side_effects=True),
    )(*pieces)


def halo_pieces(array, dx, hx, dy, hy):
    size_x, size_y = array.shape[dx], array.shape[dy]
    cut = lax.slice_in_dim
    last_x = cut(array, size_x - hx, size_x, axis=dx)
    first_x = cut(array, 0, hx, axis=dx)
    return [
        last_x,
        first_x,
        cut(array, size_y - hy, size_y, axis=dy),
        cut(array, 0, hy, axis=dy),
        cut(last_x, size_y - hy, size_y, axis=dy),
        cut(last_x, 0, hy, axis=dy),
        cut(first_x, size_y - hy, size_y, axis=dy),
        cut(first_x, 0, hy, axis=dy),
    ]


def assemble(array, dx, dy, received):
    before_x, after_x, before_y, after_y, corner_bb, corner_ba, corner_ab, corner_aa = received
    top = jnp.concatenate([corner_bb, before_x, corner_ba], axis=dy)
    mid = jnp.concatenate([before_y, array, after_y], axis=dy)
    bottom = jnp.concatenate([corner_ab, after_x, corner_aa], axis=dy)
    return jnp.concatenate([top, mid, bottom], axis=dx)


def halos(requests):
    pieces = []
    for array, dx, hx, dy, hy in requests:
        pieces += halo_pieces(array, dx, hx, dy, hy)
    received = exchange(pieces)
    count = len(OFFSETS)
    return [
        assemble(array, dx, dy, received[n * count : (n + 1) * count])
        for n, (array, dx, hx, dy, hy) in enumerate(requests)
    ]


def halo(array, dx, hx, dy, hy):
    return halos([(array, dx, hx, dy, hy)])[0]


def contract(left, right, dims, batch):
    return lax.dot_general(
        left, right, (dims, batch), precision=PREC, preferred_element_type=jnp.float32
    )


def batched_left(matrix, data):
    spread = jnp.broadcast_to(jnp.asarray(matrix), (data.shape[0],) + matrix.shape)
    return contract(spread, data, ((1,), (1,)), ((0,), (0,)))


def analyse_lead(extended):
    count = extended.shape[0] - 6
    low = 0.0
    high = 0.0
    for j in range(8):
        taken = lax.slice_in_dim(extended, j, j + count - 1, 2, 0)
        low = low + filt_low[j] * taken
        high = high + filt_high[j] * taken
    return jnp.concatenate([low, high], axis=0)


def synthesise_lead(low_ext, high_ext):
    half = low_ext.shape[0] - 4
    even = 0.0
    odd = 0.0
    for j in range(8):
        if j % 2 == 1:
            start = (3 - j) // 2 + 2
        else:
            start = (4 - j) // 2 + 2
        term = filt_low[j] * low_ext[start : start + half] + filt_high[j] * high_ext[start : start + half]
        if j % 2 == 1:
            even = even + term
        else:
            odd = odd + term
    joined = jnp.stack([even, odd], axis=1)
    return joined.reshape((2 * half,) + even.shape[1:])


def analysis_ext(extended):
    x_part = analyse_lead(extended)
    y_part = batched_left(split_analysis(x_part.shape[1] - 6), x_part)
    size_z = y_part.shape[2]
    return contract(y_part, jnp.asarray(periodic_analysis(size_z)), ((2,), (0,)), ((), ()))


def shrink_field(coeffs, thr_table, indices):
    size_x, size_y, size_z = coeffs.shape
    matched = indices[:, None] == jnp.arange(thr_table.shape[0], dtype=jnp.int32)[None, :]
    seven = jnp.sum(jnp.where(matched, thr_table[None, :], 0.0), axis=1)
    eight = jnp.concatenate([jnp.zeros((1,), jnp.float32), seven])
    high_x = (jnp.arange(size_x, dtype=jnp.int32) >= size_x // 2).astype(jnp.int32)
    high_y = (jnp.arange(size_y, dtype=jnp.int32) >= size_y // 2).astype(jnp.int32)
    high_z = (jnp.arange(size_z, dtype=jnp.int32) >= size_z // 2).astype(jnp.int32)
    band_ids = 4 * high_x[:, None, None] + 2 * high_y[None, :, None] + high_z[None, None, :]
    thresh = jnp.zeros(coeffs.shape, jnp.float32)
    for band_no in range(1, 8):
        thresh = jnp.where(band_ids == band_no, eight[band_no], thresh)
    return jnp.sign(coeffs) * jnp.maximum(jnp.abs(coeffs) - thresh, 0.0)


def synthesis_ext(extended):
    two, hx4, _, hy4, size_z = extended.shape
    z_part = contract(extended, jnp.asarray(periodic_analysis(size_z)), ((4,), (1,)), ((), ()))
    z_part = z_part.reshape(2 * hx4, 2, hy4, size_z)
    size_y = 2 * (hy4 - 4)
    matrix = split_synthesis(size_y)
    y_part = batched_left(matrix[0], z_part[:, 0]) + batched_left(matrix[1], z_part[:, 1])
    y_part = y_part.reshape(2, hx4, size_y, size_z)
    return synthesise_lead(y_part[0], y_part[1])


def blocked(cube):
    size_x, size_y, size_z = cube.shape
    return cube.reshape(2, size_x // 2, 2, size_y // 2, size_z)


def low_corner(cube):
    size_x, size_y, size_z = cube.shape
    return cube[: size_x // 2, : size_y // 2, : size_z // 2]


def local(velocity, threshold_table, band_index):
    EXCHANGE_IDS[0] = 0
    cube0 = analysis_ext(halo(velocity, 0, 3, 1, 3))
    shrunk0 = blocked(shrink_field(cube0, threshold_table, band_index[0]))
    ext1, ext0 = halos([(low_corner(cube0), 0, 9, 1, 9), (shrunk0, 1, 2, 3, 2)])
    cube1 = analysis_ext(ext1)
    shrunk1 = blocked(shrink_field(cube1, threshold_table, band_index[1]))
    cube2 = analysis_ext(low_corner(cube1))
    shrunk2 = shrink_field(cube2, threshold_table, band_index[2])
    full2 = lax.dynamic_update_slice(shrunk2, low_corner(cube2), (0, 0, 0))
    recon2 = synthesis_ext(halo(blocked(full2), 1, 4, 3, 4))
    recon2 = recon2[1 : recon2.shape[0] - 1, 1 : recon2.shape[1] - 1]
    half_z = shrunk1.shape[4] // 2
    recon1 = synthesis_ext(shrunk1.at[0, :, 0, :, :half_z].set(recon2))
    half_z = ext0.shape[4] // 2
    return synthesis_ext(ext0.at[0, :, 0, :, :half_z].set(recon1))


def solution(mesh):
    return jax.shard_map(
        local,
        mesh=mesh,
        in_specs=(P("gx", "gy", None), P(), P()),
        out_specs=P("gx", "gy", None),
        check_vma=False,
    )
```

```python
import functools

import jax
import jax.numpy as jnp
import numpy as np
from jax import lax
from jax.experimental import pallas as pl
from jax.experimental.pallas import tpu as pltpu
from jax.sharding import PartitionSpec as P

LEVELS = 3
PREC = lax.Precision.HIGH

filt_low = [
    0.23037781330885523,
    0.7148465705525415,
    0.6308807679295904,
    -0.02798376941698385,
    -0.18703481171888114,
    0.030841381835986965,
    0.032883011666982945,
    -0.010597401784997278,
]
filt_high = [(-1.0) ** j * filt_low[7 - j] for j in range(8)]


def split_analysis(length):
    matrix = np.zeros((length + 6, length), np.float32)
    for k in range(length // 2):
        for j in range(8):
            matrix[2 * k + j, k] = filt_low[j]
            matrix[2 * k + j, length // 2 + k] = filt_high[j]
    return matrix


def periodic_analysis(length):
    matrix = np.zeros((length, length), np.float32)
    for k in range(length // 2):
        for j in range(8):
            matrix[(2 * k + j - 3) % length, k] += filt_low[j]
            matrix[(2 * k + j - 3) % length, length // 2 + k] += filt_high[j]
    return matrix


def split_synthesis(length):
    half_len = length // 2
    matrix = np.zeros((2, half_len + 4, length), np.float32)
    for position in range(half_len + 4):
        k = position - 2
        for m in range(length):
            j = m + 3 - 2 * k
            if 0 <= j < 8:
                matrix[0, position, m] = filt_low[j]
                matrix[1, position, m] = filt_high[j]
    return matrix


OFFSETS = ((1, 0), (-1, 0), (0, 1), (0, -1), (1, 1), (1, -1), (-1, 1), (-1, -1))
EXCHANGE_IDS = [0]


def exchange_kernel(size_x, size_y, *refs):
    count = len(OFFSETS)
    total = (len(refs) - 2) // 2
    sources, targets = refs[:total], refs[total : 2 * total]
    send_sem, recv_sem = refs[2 * total], refs[2 * total + 1]
    me_x = lax.axis_index("gx")
    me_y = lax.axis_index("gy")
    peers = [
        (lax.rem(me_x + np.int32(dx + size_x), np.int32(size_x)), lax.rem(me_y + np.int32(dy + size_y), np.int32(size_y)))
        for dx, dy in OFFSETS
    ]
    barrier = pltpu.get_barrier_semaphore()
    for peer in peers:
        pl.semaphore_signal(barrier, inc=1, device_id=peer, device_id_type=pl.DeviceIdType.MESH)
    pl.semaphore_wait(barrier, count)
    copies = []
    for slot in range(len(sources)):
        peer = peers[slot % count]
        copy = pltpu.make_async_remote_copy(
            src_ref=sources[slot],
            dst_ref=targets[slot],
            send_sem=send_sem.at[slot],
            recv_sem=recv_sem.at[slot],
            device_id=peer,
            device_id_type=pl.DeviceIdType.MESH,
        )
        copy.start()
        copies.append(copy)
    for copy in copies:
        copy.wait()


def exchange(pieces):
    cid = EXCHANGE_IDS[0]
    EXCHANGE_IDS[0] += 1
    count = len(pieces)
    return pl.pallas_call(
        functools.partial(exchange_kernel, lax.axis_size("gx"), lax.axis_size("gy")),
        out_shape=[jax.ShapeDtypeStruct(p.shape, p.dtype) for p in pieces],
        in_specs=[pl.BlockSpec(memory_space=pl.ANY)] * count,
        out_specs=[pl.BlockSpec(memory_space=pl.ANY)] * count,
        scratch_shapes=[pltpu.SemaphoreType.DMA((count,)), pltpu.SemaphoreType.DMA((count,))],
        compiler_params=pltpu.CompilerParams(collective_id=cid, has_side_effects=True),
    )(*pieces)


def halo_pieces(array, dx, hx, dy, hy):
    size_x, size_y = array.shape[dx], array.shape[dy]
    cut = lax.slice_in_dim
    last_x = cut(array, size_x - hx, size_x, axis=dx)
    first_x = cut(array, 0, hx, axis=dx)
    return [
        last_x,
        first_x,
        cut(array, size_y - hy, size_y, axis=dy),
        cut(array, 0, hy, axis=dy),
        cut(last_x, size_y - hy, size_y, axis=dy),
        cut(last_x, 0, hy, axis=dy),
        cut(first_x, size_y - hy, size_y, axis=dy),
        cut(first_x, 0, hy, axis=dy),
    ]


def assemble(array, dx, dy, received):
    before_x, after_x, before_y, after_y, corner_bb, corner_ba, corner_ab, corner_aa = received
    top = jnp.concatenate([corner_bb, before_x, corner_ba], axis=dy)
    mid = jnp.concatenate([before_y, array, after_y], axis=dy)
    bottom = jnp.concatenate([corner_ab, after_x, corner_aa], axis=dy)
    return jnp.concatenate([top, mid, bottom], axis=dx)


def halos(requests):
    pieces = []
    for array, dx, hx, dy, hy in requests:
        pieces += halo_pieces(array, dx, hx, dy, hy)
    received = exchange(pieces)
    count = len(OFFSETS)
    return [
        assemble(array, dx, dy, received[n * count : (n + 1) * count])
        for n, (array, dx, hx, dy, hy) in enumerate(requests)
    ]


def halo(array, dx, hx, dy, hy):
    return halos([(array, dx, hx, dy, hy)])[0]


def contract(left, right, dims, batch):
    return lax.dot_general(
        left, right, (dims, batch), precision=PREC, preferred_element_type=jnp.float32
    )


def batched_left(matrix, data):
    turned = np.ascontiguousarray(matrix.T)
    spread = jnp.broadcast_to(jnp.asarray(turned), (data.shape[0],) + turned.shape)
    return contract(spread, data, ((2,), (1,)), ((0,), (0,)))


def analyse_lead(extended):
    count = extended.shape[0] - 6
    low = 0.0
    high = 0.0
    for j in range(8):
        taken = lax.slice_in_dim(extended, j, j + count - 1, 2, 0)
        low = low + filt_low[j] * taken
        high = high + filt_high[j] * taken
    return jnp.concatenate([low, high], axis=0)


def synthesise_lead(low_ext, high_ext):
    half = low_ext.shape[0] - 4
    even = 0.0
    odd = 0.0
    for j in range(8):
        if j % 2 == 1:
            start = (3 - j) // 2 + 2
        else:
            start = (4 - j) // 2 + 2
        term = filt_low[j] * low_ext[start : start + half] + filt_high[j] * high_ext[start : start + half]
        if j % 2 == 1:
            even = even + term
        else:
            odd = odd + term
    joined = jnp.stack([even, odd], axis=1)
    return joined.reshape((2 * half,) + even.shape[1:])


def analysis_ext(extended):
    x_part = analyse_lead(extended)
    y_part = batched_left(split_analysis(x_part.shape[1] - 6), x_part)
    size_z = y_part.shape[2]
    return contract(y_part, jnp.asarray(periodic_analysis(size_z)), ((2,), (0,)), ((), ()))


def shrink_field(coeffs, thr_table, indices):
    size_x, size_y, size_z = coeffs.shape
    matched = indices[:, None] == jnp.arange(thr_table.shape[0], dtype=jnp.int32)[None, :]
    seven = jnp.sum(jnp.where(matched, thr_table[None, :], 0.0), axis=1)
    eight = jnp.concatenate([jnp.zeros((1,), jnp.float32), seven])
    high_x = (jnp.arange(size_x, dtype=jnp.int32) >= size_x // 2).astype(jnp.int32)
    high_y = (jnp.arange(size_y, dtype=jnp.int32) >= size_y // 2).astype(jnp.int32)
    high_z = (jnp.arange(size_z, dtype=jnp.int32) >= size_z // 2).astype(jnp.int32)
    band_ids = 4 * high_x[:, None, None] + 2 * high_y[None, :, None] + high_z[None, None, :]
    thresh = jnp.zeros(coeffs.shape, jnp.float32)
    for band_no in range(1, 8):
        thresh = jnp.where(band_ids == band_no, eight[band_no], thresh)
    return jnp.sign(coeffs) * jnp.maximum(jnp.abs(coeffs) - thresh, 0.0)


def synthesis_ext(extended):
    two, hx4, _, hy4, size_z = extended.shape
    y_in = extended.reshape(2 * hx4, 2, hy4, size_z)
    size_y = 2 * (hy4 - 4)
    matrix = split_synthesis(size_y)
    y_part = batched_left(matrix[0], y_in[:, 0]) + batched_left(matrix[1], y_in[:, 1])
    z_part = contract(y_part, jnp.asarray(periodic_analysis(size_z)), ((2,), (1,)), ((), ()))
    z_part = z_part.reshape(2, hx4, size_y, size_z)
    return synthesise_lead(z_part[0], z_part[1])


def blocked(cube):
    size_x, size_y, size_z = cube.shape
    return cube.reshape(2, size_x // 2, 2, size_y // 2, size_z)


def low_corner(cube):
    size_x, size_y, size_z = cube.shape
    return cube[: size_x // 2, : size_y // 2, : size_z // 2]


def local(velocity, threshold_table, band_index):
    EXCHANGE_IDS[0] = 0
    cube0 = analysis_ext(halo(velocity, 0, 3, 1, 3))
    shrunk0 = blocked(shrink_field(cube0, threshold_table, band_index[0]))
    ext1, ext0 = halos([(low_corner(cube0), 0, 9, 1, 9), (shrunk0, 1, 2, 3, 2)])
    cube1 = analysis_ext(ext1)
    shrunk1 = blocked(shrink_field(cube1, threshold_table, band_index[1]))
    cube2 = analysis_ext(low_corner(cube1))
    shrunk2 = shrink_field(cube2, threshold_table, band_index[2])
    full2 = lax.dynamic_update_slice(shrunk2, low_corner(cube2), (0, 0, 0))
    recon2 = synthesis_ext(halo(blocked(full2), 1, 4, 3, 4))
    recon2 = recon2[1 : recon2.shape[0] - 1, 1 : recon2.shape[1] - 1]
    half_z = shrunk1.shape[4] // 2
    recon1 = synthesis_ext(shrunk1.at[0, :, 0, :, :half_z].set(recon2))
    half_z = ext0.shape[4] // 2
    return synthesis_ext(ext0.at[0, :, 0, :, :half_z].set(recon1))


def solution(mesh):
    return jax.shard_map(
        local,
        mesh=mesh,
        in_specs=(P("gx", "gy", None), P(), P()),
        out_specs=P("gx", "gy", None),
        check_vma=False,
    )
```

```python
import functools

import jax
import jax.numpy as jnp
import numpy as np
from jax import lax
from jax.experimental import pallas as pl
from jax.experimental.pallas import tpu as pltpu
from jax.sharding import PartitionSpec as P

LEVELS = 3
PREC = lax.Precision.HIGH

filt_low = [
    0.23037781330885523,
    0.7148465705525415,
    0.6308807679295904,
    -0.02798376941698385,
    -0.18703481171888114,
    0.030841381835986965,
    0.032883011666982945,
    -0.010597401784997278,
]
filt_high = [(-1.0) ** j * filt_low[7 - j] for j in range(8)]


def split_analysis(length):
    matrix = np.zeros((length + 6, length), np.float32)
    for k in range(length // 2):
        for j in range(8):
            matrix[2 * k + j, k] = filt_low[j]
            matrix[2 * k + j, length // 2 + k] = filt_high[j]
    return matrix


def periodic_analysis(length):
    matrix = np.zeros((length, length), np.float32)
    for k in range(length // 2):
        for j in range(8):
            matrix[(2 * k + j - 3) % length, k] += filt_low[j]
            matrix[(2 * k + j - 3) % length, length // 2 + k] += filt_high[j]
    return matrix


def split_synthesis(length):
    half_len = length // 2
    matrix = np.zeros((2, half_len + 4, length), np.float32)
    for position in range(half_len + 4):
        k = position - 2
        for m in range(length):
            j = m + 3 - 2 * k
            if 0 <= j < 8:
                matrix[0, position, m] = filt_low[j]
                matrix[1, position, m] = filt_high[j]
    return matrix


OFFSETS = ((1, 0), (-1, 0), (0, 1), (0, -1), (1, 1), (1, -1), (-1, 1), (-1, -1))
EXCHANGE_IDS = [0]


def windows(offset, size, halo_len):
    if offset == 1:
        return size - halo_len, halo_len
    if offset == -1:
        return 0, halo_len
    return 0, size


def exchange_kernel(layouts, mesh_x, mesh_y, *refs):
    count = len(OFFSETS)
    arrays = len(layouts)
    sources = refs[:arrays]
    targets = refs[arrays : arrays + arrays * count]
    send_sem, recv_sem = refs[arrays + arrays * count], refs[arrays + arrays * count + 1]
    me_x = lax.axis_index("gx")
    me_y = lax.axis_index("gy")
    peers = [
        (lax.rem(me_x + np.int32(ox + mesh_x), np.int32(mesh_x)), lax.rem(me_y + np.int32(oy + mesh_y), np.int32(mesh_y)))
        for ox, oy in OFFSETS
    ]
    barrier = pltpu.get_barrier_semaphore()
    for peer in peers:
        pl.semaphore_signal(barrier, inc=1, device_id=peer, device_id_type=pl.DeviceIdType.MESH)
    pl.semaphore_wait(barrier, count)
    copies = []
    for n, (ndim, dx, hx, size_x, dy, hy, size_y) in enumerate(layouts):
        for s, ((ox, oy), peer) in enumerate(zip(OFFSETS, peers)):
            index = [slice(None)] * ndim
            index[dx] = pl.ds(*windows(ox, size_x, hx))
            index[dy] = pl.ds(*windows(oy, size_y, hy))
            slot = n * count + s
            copy = pltpu.make_async_remote_copy(
                src_ref=sources[n].at[tuple(index)],
                dst_ref=targets[slot],
                send_sem=send_sem.at[slot],
                recv_sem=recv_sem.at[slot],
                device_id=peer,
                device_id_type=pl.DeviceIdType.MESH,
            )
            copy.start()
            copies.append(copy)
    for copy in copies:
        copy.wait()


def piece_shape(array, dx, hx, dy, hy, offset):
    shape = list(array.shape)
    shape[dx] = windows(offset[0], shape[dx], hx)[1]
    shape[dy] = windows(offset[1], shape[dy], hy)[1]
    return jax.ShapeDtypeStruct(tuple(shape), array.dtype)


def halos(requests):
    cid = EXCHANGE_IDS[0]
    EXCHANGE_IDS[0] += 1
    count = len(OFFSETS)
    layouts = tuple(
        (array.ndim, dx, hx, array.shape[dx], dy, hy, array.shape[dy]) for array, dx, hx, dy, hy in requests
    )
    shapes = [piece_shape(array, dx, hx, dy, hy, offset) for array, dx, hx, dy, hy in requests for offset in OFFSETS]
    received = pl.pallas_call(
        functools.partial(exchange_kernel, layouts, lax.axis_size("gx"), lax.axis_size("gy")),
        out_shape=shapes,
        in_specs=[pl.BlockSpec(memory_space=pl.ANY)] * len(requests),
        out_specs=[pl.BlockSpec(memory_space=pl.ANY)] * len(shapes),
        scratch_shapes=[pltpu.SemaphoreType.DMA((len(shapes),)), pltpu.SemaphoreType.DMA((len(shapes),))],
        compiler_params=pltpu.CompilerParams(collective_id=cid, has_side_effects=True),
    )(*[request[0] for request in requests])
    return [
        assemble(array, dx, dy, received[n * count : (n + 1) * count])
        for n, (array, dx, hx, dy, hy) in enumerate(requests)
    ]


def assemble(array, dx, dy, received):
    before_x, after_x, before_y, after_y, corner_bb, corner_ba, corner_ab, corner_aa = received
    top = jnp.concatenate([corner_bb, before_x, corner_ba], axis=dy)
    mid = jnp.concatenate([before_y, array, after_y], axis=dy)
    bottom = jnp.concatenate([corner_ab, after_x, corner_aa], axis=dy)
    return jnp.concatenate([top, mid, bottom], axis=dx)


def halo(array, dx, hx, dy, hy):
    return halos([(array, dx, hx, dy, hy)])[0]


def contract(left, right, dims, batch):
    return lax.dot_general(
        left, right, (dims, batch), precision=PREC, preferred_element_type=jnp.float32
    )


def batched_left(matrix, data):
    spread = jnp.broadcast_to(jnp.asarray(matrix), (data.shape[0],) + matrix.shape)
    return contract(spread, data, ((1,), (1,)), ((0,), (0,)))


def analyse_lead(extended):
    count = extended.shape[0] - 6
    low = 0.0
    high = 0.0
    for j in range(8):
        taken = lax.slice_in_dim(extended, j, j + count - 1, 2, 0)
        low = low + filt_low[j] * taken
        high = high + filt_high[j] * taken
    return jnp.concatenate([low, high], axis=0)


def synthesise_lead(low_ext, high_ext):
    half = low_ext.shape[0] - 4
    even = 0.0
    odd = 0.0
    for j in range(8):
        if j % 2 == 1:
            start = (3 - j) // 2 + 2
        else:
            start = (4 - j) // 2 + 2
        term = filt_low[j] * low_ext[start : start + half] + filt_high[j] * high_ext[start : start + half]
        if j % 2 == 1:
            even = even + term
        else:
            odd = odd + term
    joined = jnp.stack([even, odd], axis=1)
    return joined.reshape((2 * half,) + even.shape[1:])


def analysis_ext(extended):
    x_part = analyse_lead(extended)
    y_part = batched_left(split_analysis(x_part.shape[1] - 6), x_part)
    size_z = y_part.shape[2]
    return contract(y_part, jnp.asarray(periodic_analysis(size_z)), ((2,), (0,)), ((), ()))


def shrink_field(coeffs, thr_table, indices):
    size_x, size_y, size_z = coeffs.shape
    matched = indices[:, None] == jnp.arange(thr_table.shape[0], dtype=jnp.int32)[None, :]
    seven = jnp.sum(jnp.where(matched, thr_table[None, :], 0.0), axis=1)
    eight = jnp.concatenate([jnp.zeros((1,), jnp.float32), seven])
    high_x = (jnp.arange(size_x, dtype=jnp.int32) >= size_x // 2).astype(jnp.int32)
    high_y = (jnp.arange(size_y, dtype=jnp.int32) >= size_y // 2).astype(jnp.int32)
    high_z = (jnp.arange(size_z, dtype=jnp.int32) >= size_z // 2).astype(jnp.int32)
    band_ids = 4 * high_x[:, None, None] + 2 * high_y[None, :, None] + high_z[None, None, :]
    thresh = jnp.zeros(coeffs.shape, jnp.float32)
    for band_no in range(1, 8):
        thresh = jnp.where(band_ids == band_no, eight[band_no], thresh)
    return jnp.sign(coeffs) * jnp.maximum(jnp.abs(coeffs) - thresh, 0.0)


def synthesis_ext(extended):
    two, hx4, _, hy4, size_z = extended.shape
    z_part = contract(extended, jnp.asarray(periodic_analysis(size_z)), ((4,), (1,)), ((), ()))
    z_part = z_part.reshape(2 * hx4, 2, hy4, size_z)
    size_y = 2 * (hy4 - 4)
    matrix = split_synthesis(size_y)
    y_part = batched_left(matrix[0], z_part[:, 0]) + batched_left(matrix[1], z_part[:, 1])
    y_part = y_part.reshape(2, hx4, size_y, size_z)
    return synthesise_lead(y_part[0], y_part[1])


def blocked(cube):
    size_x, size_y, size_z = cube.shape
    return cube.reshape(2, size_x // 2, 2, size_y // 2, size_z)


def low_corner(cube):
    size_x, size_y, size_z = cube.shape
    return cube[: size_x // 2, : size_y // 2, : size_z // 2]


def local(velocity, threshold_table, band_index):
    EXCHANGE_IDS[0] = 0
    cube0 = analysis_ext(halo(velocity, 0, 3, 1, 3))
    shrunk0 = blocked(shrink_field(cube0, threshold_table, band_index[0]))
    ext1, ext0 = halos([(low_corner(cube0), 0, 9, 1, 9), (shrunk0, 1, 2, 3, 2)])
    cube1 = analysis_ext(ext1)
    shrunk1 = blocked(shrink_field(cube1, threshold_table, band_index[1]))
    cube2 = analysis_ext(low_corner(cube1))
    shrunk2 = shrink_field(cube2, threshold_table, band_index[2])
    full2 = lax.dynamic_update_slice(shrunk2, low_corner(cube2), (0, 0, 0))
    recon2 = synthesis_ext(halo(blocked(full2), 1, 4, 3, 4))
    recon2 = recon2[1 : recon2.shape[0] - 1, 1 : recon2.shape[1] - 1]
    half_z = shrunk1.shape[4] // 2
    recon1 = synthesis_ext(shrunk1.at[0, :, 0, :, :half_z].set(recon2))
    half_z = ext0.shape[4] // 2
    return synthesis_ext(ext0.at[0, :, 0, :, :half_z].set(recon1))


def solution(mesh):
    return jax.shard_map(
        local,
        mesh=mesh,
        in_specs=(P("gx", "gy", None), P(), P()),
        out_specs=P("gx", "gy", None),
        check_vma=False,
    )
```

```python
import functools

import jax
import jax.numpy as jnp
import numpy as np
from jax import lax
from jax.experimental import pallas as pl
from jax.experimental.pallas import tpu as pltpu
from jax.sharding import PartitionSpec as P

LEVELS = 3
PREC = lax.Precision.HIGH

filt_low = [
    0.23037781330885523,
    0.7148465705525415,
    0.6308807679295904,
    -0.02798376941698385,
    -0.18703481171888114,
    0.030841381835986965,
    0.032883011666982945,
    -0.010597401784997278,
]
filt_high = [(-1.0) ** j * filt_low[7 - j] for j in range(8)]


def split_analysis(length):
    matrix = np.zeros((length + 6, length), np.float32)
    for k in range(length // 2):
        for j in range(8):
            matrix[2 * k + j, k] = filt_low[j]
            matrix[2 * k + j, length // 2 + k] = filt_high[j]
    return matrix


def periodic_analysis(length):
    matrix = np.zeros((length, length), np.float32)
    for k in range(length // 2):
        for j in range(8):
            matrix[(2 * k + j - 3) % length, k] += filt_low[j]
            matrix[(2 * k + j - 3) % length, length // 2 + k] += filt_high[j]
    return matrix


def split_synthesis(length):
    half_len = length // 2
    matrix = np.zeros((2, half_len + 4, length), np.float32)
    for position in range(half_len + 4):
        k = position - 2
        for m in range(length):
            j = m + 3 - 2 * k
            if 0 <= j < 8:
                matrix[0, position, m] = filt_low[j]
                matrix[1, position, m] = filt_high[j]
    return matrix


OFFSETS = ((1, 0), (-1, 0), (0, 1), (0, -1), (1, 1), (1, -1), (-1, 1), (-1, -1))
EXCHANGE_IDS = [0]


def windows(offset, size, halo_len):
    if offset == 1:
        return size - halo_len, halo_len
    if offset == -1:
        return 0, halo_len
    return 0, size


def exchange_kernel(layouts, mesh_x, mesh_y, *refs):
    count = len(OFFSETS)
    arrays = len(layouts)
    sources = refs[:arrays]
    targets = refs[arrays : arrays + arrays * count]
    send_sem, recv_sem = refs[arrays + arrays * count], refs[arrays + arrays * count + 1]
    me_x = lax.axis_index("gx")
    me_y = lax.axis_index("gy")
    peers = [
        (lax.rem(me_x + np.int32(ox + mesh_x), np.int32(mesh_x)), lax.rem(me_y + np.int32(oy + mesh_y), np.int32(mesh_y)))
        for ox, oy in OFFSETS
    ]
    barrier = pltpu.get_barrier_semaphore()
    for peer in peers:
        pl.semaphore_signal(barrier, inc=1, device_id=peer, device_id_type=pl.DeviceIdType.MESH)
    pl.semaphore_wait(barrier, count)
    copies = []
    for n, (ndim, dx, hx, size_x, dy, hy, size_y) in enumerate(layouts):
        for s, ((ox, oy), peer) in enumerate(zip(OFFSETS, peers)):
            index = [slice(None)] * ndim
            index[dx] = pl.ds(*windows(ox, size_x, hx))
            index[dy] = pl.ds(*windows(oy, size_y, hy))
            slot = n * count + s
            copy = pltpu.make_async_remote_copy(
                src_ref=sources[n].at[tuple(index)],
                dst_ref=targets[slot],
                send_sem=send_sem.at[slot],
                recv_sem=recv_sem.at[slot],
                device_id=peer,
                device_id_type=pl.DeviceIdType.MESH,
            )
            copy.start()
            copies.append(copy)
    for copy in copies:
        copy.wait()


def piece_shape(array, dx, hx, dy, hy, offset):
    shape = list(array.shape)
    shape[dx] = windows(offset[0], shape[dx], hx)[1]
    shape[dy] = windows(offset[1], shape[dy], hy)[1]
    return jax.ShapeDtypeStruct(tuple(shape), array.dtype)


def halos(requests):
    cid = EXCHANGE_IDS[0]
    EXCHANGE_IDS[0] += 1
    count = len(OFFSETS)
    layouts = tuple(
        (array.ndim, dx, hx, array.shape[dx], dy, hy, array.shape[dy]) for array, dx, hx, dy, hy in requests
    )
    shapes = [piece_shape(array, dx, hx, dy, hy, offset) for array, dx, hx, dy, hy in requests for offset in OFFSETS]
    received = pl.pallas_call(
        functools.partial(exchange_kernel, layouts, lax.axis_size("gx"), lax.axis_size("gy")),
        out_shape=shapes,
        in_specs=[pl.BlockSpec(memory_space=pl.ANY)] * len(requests),
        out_specs=[pl.BlockSpec(memory_space=pl.ANY)] * len(shapes),
        scratch_shapes=[pltpu.SemaphoreType.DMA((len(shapes),)), pltpu.SemaphoreType.DMA((len(shapes),))],
        compiler_params=pltpu.CompilerParams(collective_id=cid, has_side_effects=True),
    )(*[request[0] for request in requests])
    return [
        assemble(array, dx, dy, received[n * count : (n + 1) * count])
        for n, (array, dx, hx, dy, hy) in enumerate(requests)
    ]


def assemble(array, dx, dy, received):
    before_x, after_x, before_y, after_y, corner_bb, corner_ba, corner_ab, corner_aa = received
    top = jnp.concatenate([corner_bb, before_x, corner_ba], axis=dy)
    mid = jnp.concatenate([before_y, array, after_y], axis=dy)
    bottom = jnp.concatenate([corner_ab, after_x, corner_aa], axis=dy)
    return jnp.concatenate([top, mid, bottom], axis=dx)


def halo(array, dx, hx, dy, hy):
    return halos([(array, dx, hx, dy, hy)])[0]


def contract(left, right, dims, batch):
    return lax.dot_general(
        left, right, (dims, batch), precision=PREC, preferred_element_type=jnp.float32
    )


def batched_left(matrix, data):
    spread = jnp.broadcast_to(jnp.asarray(matrix), (data.shape[0],) + matrix.shape)
    return contract(spread, data, ((1,), (1,)), ((0,), (0,)))


def analyse_lead(extended):
    count = extended.shape[0] - 6
    low = 0.0
    high = 0.0
    for j in range(8):
        taken = lax.slice_in_dim(extended, j, j + count - 1, 2, 0)
        low = low + filt_low[j] * taken
        high = high + filt_high[j] * taken
    return jnp.concatenate([low, high], axis=0)


def synthesise_lead(low_ext, high_ext):
    half = low_ext.shape[0] - 4
    even = 0.0
    odd = 0.0
    for j in range(8):
        if j % 2 == 1:
            start = (3 - j) // 2 + 2
        else:
            start = (4 - j) // 2 + 2
        term = filt_low[j] * low_ext[start : start + half] + filt_high[j] * high_ext[start : start + half]
        if j % 2 == 1:
            even = even + term
        else:
            odd = odd + term
    joined = jnp.stack([even, odd], axis=1)
    return joined.reshape((2 * half,) + even.shape[1:])


def analysis_ext(extended):
    x_part = analyse_lead(extended)
    y_part = batched_left(split_analysis(x_part.shape[1] - 6), x_part)
    size_z = y_part.shape[2]
    return contract(y_part, jnp.asarray(periodic_analysis(size_z)), ((2,), (0,)), ((), ()))


def shrink_field(coeffs, thr_table, indices):
    size_x, size_y, size_z = coeffs.shape
    matched = indices[:, None] == jnp.arange(thr_table.shape[0], dtype=jnp.int32)[None, :]
    seven = jnp.sum(jnp.where(matched, thr_table[None, :], 0.0), axis=1)
    eight = jnp.concatenate([jnp.zeros((1,), jnp.float32), seven])
    high_x = (jnp.arange(size_x, dtype=jnp.int32) >= size_x // 2).astype(jnp.int32)
    high_y = (jnp.arange(size_y, dtype=jnp.int32) >= size_y // 2).astype(jnp.int32)
    high_z = (jnp.arange(size_z, dtype=jnp.int32) >= size_z // 2).astype(jnp.int32)
    band_ids = 4 * high_x[:, None, None] + 2 * high_y[None, :, None] + high_z[None, None, :]
    thresh = jnp.zeros(coeffs.shape, jnp.float32)
    for band_no in range(1, 8):
        thresh = jnp.where(band_ids == band_no, eight[band_no], thresh)
    return jnp.sign(coeffs) * jnp.maximum(jnp.abs(coeffs) - thresh, 0.0)


def synthesis_ext(extended):
    two, hx4, _, hy4, size_z = extended.shape
    z_part = contract(extended, jnp.asarray(periodic_analysis(size_z)), ((4,), (1,)), ((), ()))
    z_part = z_part.reshape(2 * hx4, 2, hy4, size_z)
    size_y = 2 * (hy4 - 4)
    matrix = split_synthesis(size_y)
    y_part = batched_left(matrix[0], z_part[:, 0]) + batched_left(matrix[1], z_part[:, 1])
    y_part = y_part.reshape(2, hx4, size_y, size_z)
    return synthesise_lead(y_part[0], y_part[1])


def split_bf16(values):
    high = values.astype(jnp.bfloat16)
    low = (values - high.astype(jnp.float32)).astype(jnp.bfloat16)
    return high, low


def synth_yx_kernel(matrix_ref, in_ref, out_ref, rows_ref):
    n_rows = in_ref.shape[0]
    hx4 = n_rows // 2
    half = hx4 - 4

    def y_row(r, carry):
        total = None
        for band in range(2):
            high, low = split_bf16(in_ref[r, band])
            m_high = matrix_ref[band, 0]
            m_low = matrix_ref[band, 1]
            part = jnp.dot(m_high, high, preferred_element_type=jnp.float32)
            part = part + jnp.dot(m_high, low, preferred_element_type=jnp.float32)
            part = part + jnp.dot(m_low, high, preferred_element_type=jnp.float32)
            total = part if total is None else total + part
        rows_ref[r] = total
        return carry

    lax.fori_loop(0, n_rows, y_row, 0)

    def x_row(q, carry):
        even = None
        odd = None
        for j in range(8):
            start = (3 - j) // 2 + 2 if j % 2 == 1 else (4 - j) // 2 + 2
            term = filt_low[j] * rows_ref[q + start] + filt_high[j] * rows_ref[hx4 + q + start]
            if j % 2 == 1:
                even = term if even is None else even + term
            else:
                odd = term if odd is None else odd + term
        out_ref[2 * q] = even
        out_ref[2 * q + 1] = odd
        return carry

    lax.fori_loop(0, half, x_row, 0)


def synthesis_yx(z_part, size_y):
    n_rows, _, hy4, size_z = z_part.shape
    matrix = split_synthesis(size_y)
    turned = np.ascontiguousarray(np.transpose(matrix, (0, 2, 1)))
    m_high = turned.astype(jnp.bfloat16)
    m_low = (turned - m_high.astype(np.float32)).astype(jnp.bfloat16)
    parts = jnp.asarray(np.stack([m_high, m_low], axis=1))
    block_z = 128
    size_x = 2 * (n_rows // 2 - 4)
    return pl.pallas_call(
        synth_yx_kernel,
        grid=(size_z // block_z,),
        in_specs=[
            pl.BlockSpec(parts.shape, lambda i: (0, 0, 0, 0)),
            pl.BlockSpec((n_rows, 2, hy4, block_z), lambda i: (0, 0, 0, i)),
        ],
        out_specs=pl.BlockSpec((size_x, size_y, block_z), lambda i: (0, 0, i)),
        out_shape=jax.ShapeDtypeStruct((size_x, size_y, size_z), jnp.float32),
        scratch_shapes=[pltpu.VMEM((n_rows, size_y, block_z), jnp.float32)],
    )(parts, z_part)


def synthesis_level0(extended):
    two, hx4, _, hy4, size_z = extended.shape
    z_part = contract(extended, jnp.asarray(periodic_analysis(size_z)), ((4,), (1,)), ((), ()))
    return synthesis_yx(z_part.reshape(2 * hx4, 2, hy4, size_z), 2 * (hy4 - 4))


def blocked(cube):
    size_x, size_y, size_z = cube.shape
    return cube.reshape(2, size_x // 2, 2, size_y // 2, size_z)


def low_corner(cube):
    size_x, size_y, size_z = cube.shape
    return cube[: size_x // 2, : size_y // 2, : size_z // 2]


def local(velocity, threshold_table, band_index):
    EXCHANGE_IDS[0] = 0
    cube0 = analysis_ext(halo(velocity, 0, 3, 1, 3))
    shrunk0 = blocked(shrink_field(cube0, threshold_table, band_index[0]))
    ext1, ext0 = halos([(low_corner(cube0), 0, 9, 1, 9), (shrunk0, 1, 2, 3, 2)])
    cube1 = analysis_ext(ext1)
    shrunk1 = blocked(shrink_field(cube1, threshold_table, band_index[1]))
    cube2 = analysis_ext(low_corner(cube1))
    shrunk2 = shrink_field(cube2, threshold_table, band_index[2])
    full2 = lax.dynamic_update_slice(shrunk2, low_corner(cube2), (0, 0, 0))
    recon2 = synthesis_ext(halo(blocked(full2), 1, 4, 3, 4))
    recon2 = recon2[1 : recon2.shape[0] - 1, 1 : recon2.shape[1] - 1]
    half_z = shrunk1.shape[4] // 2
    recon1 = synthesis_ext(shrunk1.at[0, :, 0, :, :half_z].set(recon2))
    half_z = ext0.shape[4] // 2
    return synthesis_level0(ext0.at[0, :, 0, :, :half_z].set(recon1))


def solution(mesh):
    return jax.shard_map(
        local,
        mesh=mesh,
        in_specs=(P("gx", "gy", None), P(), P()),
        out_specs=P("gx", "gy", None),
        check_vma=False,
    )
```

```python
import functools

import jax
import jax.numpy as jnp
import numpy as np
from jax import lax
from jax.experimental import pallas as pl
from jax.experimental.pallas import tpu as pltpu
from jax.sharding import PartitionSpec as P

LEVELS = 3
PREC = lax.Precision.HIGH

filt_low = [
    0.23037781330885523,
    0.7148465705525415,
    0.6308807679295904,
    -0.02798376941698385,
    -0.18703481171888114,
    0.030841381835986965,
    0.032883011666982945,
    -0.010597401784997278,
]
filt_high = [(-1.0) ** j * filt_low[7 - j] for j in range(8)]


def split_analysis(length):
    matrix = np.zeros((length + 6, length), np.float32)
    for k in range(length // 2):
        for j in range(8):
            matrix[2 * k + j, k] = filt_low[j]
            matrix[2 * k + j, length // 2 + k] = filt_high[j]
    return matrix


def periodic_analysis(length):
    matrix = np.zeros((length, length), np.float32)
    for k in range(length // 2):
        for j in range(8):
            matrix[(2 * k + j - 3) % length, k] += filt_low[j]
            matrix[(2 * k + j - 3) % length, length // 2 + k] += filt_high[j]
    return matrix


def split_synthesis(length):
    half_len = length // 2
    matrix = np.zeros((2, half_len + 4, length), np.float32)
    for position in range(half_len + 4):
        k = position - 2
        for m in range(length):
            j = m + 3 - 2 * k
            if 0 <= j < 8:
                matrix[0, position, m] = filt_low[j]
                matrix[1, position, m] = filt_high[j]
    return matrix


OFFSETS = ((1, 0), (-1, 0), (0, 1), (0, -1), (1, 1), (1, -1), (-1, 1), (-1, -1))
EXCHANGE_IDS = [0]


def windows(offset, size, halo_len):
    if offset == 1:
        return size - halo_len, halo_len
    if offset == -1:
        return 0, halo_len
    return 0, size


def exchange_kernel(layouts, mesh_x, mesh_y, *refs):
    count = len(OFFSETS)
    arrays = len(layouts)
    sources = refs[:arrays]
    targets = refs[arrays : arrays + arrays * count]
    send_sem, recv_sem = refs[arrays + arrays * count], refs[arrays + arrays * count + 1]
    me_x = lax.axis_index("gx")
    me_y = lax.axis_index("gy")
    peers = [
        (lax.rem(me_x + np.int32(ox + mesh_x), np.int32(mesh_x)), lax.rem(me_y + np.int32(oy + mesh_y), np.int32(mesh_y)))
        for ox, oy in OFFSETS
    ]
    barrier = pltpu.get_barrier_semaphore()
    for peer in peers:
        pl.semaphore_signal(barrier, inc=1, device_id=peer, device_id_type=pl.DeviceIdType.MESH)
    pl.semaphore_wait(barrier, count)
    copies = []
    for n, (ndim, dx, hx, size_x, dy, hy, size_y) in enumerate(layouts):
        for s, ((ox, oy), peer) in enumerate(zip(OFFSETS, peers)):
            index = [slice(None)] * ndim
            index[dx] = pl.ds(*windows(ox, size_x, hx))
            index[dy] = pl.ds(*windows(oy, size_y, hy))
            slot = n * count + s
            copy = pltpu.make_async_remote_copy(
                src_ref=sources[n].at[tuple(index)],
                dst_ref=targets[slot],
                send_sem=send_sem.at[slot],
                recv_sem=recv_sem.at[slot],
                device_id=peer,
                device_id_type=pl.DeviceIdType.MESH,
            )
            copy.start()
            copies.append(copy)
    for copy in copies:
        copy.wait()


def piece_shape(array, dx, hx, dy, hy, offset):
    shape = list(array.shape)
    shape[dx] = windows(offset[0], shape[dx], hx)[1]
    shape[dy] = windows(offset[1], shape[dy], hy)[1]
    return jax.ShapeDtypeStruct(tuple(shape), array.dtype)


def halos(requests):
    cid = EXCHANGE_IDS[0]
    EXCHANGE_IDS[0] += 1
    count = len(OFFSETS)
    layouts = tuple(
        (array.ndim, dx, hx, array.shape[dx], dy, hy, array.shape[dy]) for array, dx, hx, dy, hy in requests
    )
    shapes = [piece_shape(array, dx, hx, dy, hy, offset) for array, dx, hx, dy, hy in requests for offset in OFFSETS]
    received = pl.pallas_call(
        functools.partial(exchange_kernel, layouts, lax.axis_size("gx"), lax.axis_size("gy")),
        out_shape=shapes,
        in_specs=[pl.BlockSpec(memory_space=pl.ANY)] * len(requests),
        out_specs=[pl.BlockSpec(memory_space=pl.ANY)] * len(shapes),
        scratch_shapes=[pltpu.SemaphoreType.DMA((len(shapes),)), pltpu.SemaphoreType.DMA((len(shapes),))],
        compiler_params=pltpu.CompilerParams(collective_id=cid, has_side_effects=True),
    )(*[request[0] for request in requests])
    return [
        assemble(array, dx, dy, received[n * count : (n + 1) * count])
        for n, (array, dx, hx, dy, hy) in enumerate(requests)
    ]


def assemble(array, dx, dy, received):
    before_x, after_x, before_y, after_y, corner_bb, corner_ba, corner_ab, corner_aa = received
    top = jnp.concatenate([corner_bb, before_x, corner_ba], axis=dy)
    mid = jnp.concatenate([before_y, array, after_y], axis=dy)
    bottom = jnp.concatenate([corner_ab, after_x, corner_aa], axis=dy)
    return jnp.concatenate([top, mid, bottom], axis=dx)


def halo(array, dx, hx, dy, hy):
    return halos([(array, dx, hx, dy, hy)])[0]


def contract(left, right, dims, batch):
    return lax.dot_general(
        left, right, (dims, batch), precision=PREC, preferred_element_type=jnp.float32
    )


def batched_left(matrix, data):
    spread = jnp.broadcast_to(jnp.asarray(matrix), (data.shape[0],) + matrix.shape)
    return contract(spread, data, ((1,), (1,)), ((0,), (0,)))


def analyse_lead(extended):
    count = extended.shape[0] - 6
    low = 0.0
    high = 0.0
    for j in range(8):
        taken = lax.slice_in_dim(extended, j, j + count - 1, 2, 0)
        low = low + filt_low[j] * taken
        high = high + filt_high[j] * taken
    return jnp.concatenate([low, high], axis=0)


def synthesise_lead(low_ext, high_ext):
    half = low_ext.shape[0] - 4
    even = 0.0
    odd = 0.0
    for j in range(8):
        if j % 2 == 1:
            start = (3 - j) // 2 + 2
        else:
            start = (4 - j) // 2 + 2
        term = filt_low[j] * low_ext[start : start + half] + filt_high[j] * high_ext[start : start + half]
        if j % 2 == 1:
            even = even + term
        else:
            odd = odd + term
    joined = jnp.stack([even, odd], axis=1)
    return joined.reshape((2 * half,) + even.shape[1:])


def analysis_ext(extended):
    x_part = analyse_lead(extended)
    y_part = batched_left(split_analysis(x_part.shape[1] - 6), x_part)
    size_x, size_y, size_z = y_part.shape
    matrix = jnp.asarray(periodic_analysis(size_z))
    if size_y % 8 == 0:
        flat = contract(y_part.reshape(size_x * size_y, size_z), matrix, ((1,), (0,)), ((), ()))
        return flat.reshape(size_x, size_y, size_z)
    return contract(y_part, matrix, ((2,), (0,)), ((), ()))


def shrink_field(coeffs, thr_table, indices):
    size_x, size_y, size_z = coeffs.shape
    matched = indices[:, None] == jnp.arange(thr_table.shape[0], dtype=jnp.int32)[None, :]
    seven = jnp.sum(jnp.where(matched, thr_table[None, :], 0.0), axis=1)
    eight = jnp.concatenate([jnp.zeros((1,), jnp.float32), seven])
    high_x = (jnp.arange(size_x, dtype=jnp.int32) >= size_x // 2).astype(jnp.int32)
    high_y = (jnp.arange(size_y, dtype=jnp.int32) >= size_y // 2).astype(jnp.int32)
    plane_ids = 4 * high_x[:, None] + 2 * high_y[None, :]
    low_z = jnp.zeros((size_x, size_y), jnp.float32)
    high_z = jnp.zeros((size_x, size_y), jnp.float32)
    for band_no in range(1, 8):
        if band_no % 2 == 0:
            low_z = jnp.where(plane_ids == band_no, eight[band_no], low_z)
        else:
            high_z = jnp.where(plane_ids + 1 == band_no, eight[band_no], high_z)
    in_high = (jnp.arange(size_z, dtype=jnp.int32) >= size_z // 2)[None, None, :]
    thresh = jnp.where(in_high, high_z[:, :, None], low_z[:, :, None])
    return jnp.sign(coeffs) * jnp.maximum(jnp.abs(coeffs) - thresh, 0.0)


def synthesis_ext(extended):
    two, hx4, _, hy4, size_z = extended.shape
    z_part = contract(extended, jnp.asarray(periodic_analysis(size_z)), ((4,), (1,)), ((), ()))
    z_part = z_part.reshape(2 * hx4, 2, hy4, size_z)
    size_y = 2 * (hy4 - 4)
    matrix = split_synthesis(size_y)
    y_part = batched_left(matrix[0], z_part[:, 0]) + batched_left(matrix[1], z_part[:, 1])
    y_part = y_part.reshape(2, hx4, size_y, size_z)
    return synthesise_lead(y_part[0], y_part[1])


def blocked(cube):
    size_x, size_y, size_z = cube.shape
    return cube.reshape(2, size_x // 2, 2, size_y // 2, size_z)


def low_corner(cube):
    size_x, size_y, size_z = cube.shape
    return cube[: size_x // 2, : size_y // 2, : size_z // 2]


def local(velocity, threshold_table, band_index):
    EXCHANGE_IDS[0] = 0
    cube0 = analysis_ext(halo(velocity, 0, 3, 1, 3))
    shrunk0 = blocked(shrink_field(cube0, threshold_table, band_index[0]))
    ext1, ext0 = halos([(low_corner(cube0), 0, 9, 1, 9), (shrunk0, 1, 2, 3, 2)])
    cube1 = analysis_ext(ext1)
    shrunk1 = blocked(shrink_field(cube1, threshold_table, band_index[1]))
    cube2 = analysis_ext(low_corner(cube1))
    shrunk2 = shrink_field(cube2, threshold_table, band_index[2])
    full2 = lax.dynamic_update_slice(shrunk2, low_corner(cube2), (0, 0, 0))
    recon2 = synthesis_ext(halo(blocked(full2), 1, 4, 3, 4))
    recon2 = recon2[1 : recon2.shape[0] - 1, 1 : recon2.shape[1] - 1]
    half_z = shrunk1.shape[4] // 2
    recon1 = synthesis_ext(shrunk1.at[0, :, 0, :, :half_z].set(recon2))
    half_z = ext0.shape[4] // 2
    return synthesis_ext(ext0.at[0, :, 0, :, :half_z].set(recon1))


def solution(mesh):
    return jax.shard_map(
        local,
        mesh=mesh,
        in_specs=(P("gx", "gy", None), P(), P()),
        out_specs=P("gx", "gy", None),
        check_vma=False,
    )
```

```python
import functools

import jax
import jax.numpy as jnp
import numpy as np
from jax import lax
from jax.experimental import pallas as pl
from jax.experimental.pallas import tpu as pltpu
from jax.sharding import PartitionSpec as P

LEVELS = 3
PREC = lax.Precision.HIGH

filt_low = [
    0.23037781330885523,
    0.7148465705525415,
    0.6308807679295904,
    -0.02798376941698385,
    -0.18703481171888114,
    0.030841381835986965,
    0.032883011666982945,
    -0.010597401784997278,
]
filt_high = [(-1.0) ** j * filt_low[7 - j] for j in range(8)]


def split_analysis(length):
    matrix = np.zeros((length + 6, length), np.float32)
    for k in range(length // 2):
        for j in range(8):
            matrix[2 * k + j, k] = filt_low[j]
            matrix[2 * k + j, length // 2 + k] = filt_high[j]
    return matrix


def periodic_analysis(length):
    matrix = np.zeros((length, length), np.float32)
    for k in range(length // 2):
        for j in range(8):
            matrix[(2 * k + j - 3) % length, k] += filt_low[j]
            matrix[(2 * k + j - 3) % length, length // 2 + k] += filt_high[j]
    return matrix


def split_synthesis(length):
    half_len = length // 2
    matrix = np.zeros((2, half_len + 4, length), np.float32)
    for position in range(half_len + 4):
        k = position - 2
        for m in range(length):
            j = m + 3 - 2 * k
            if 0 <= j < 8:
                matrix[0, position, m] = filt_low[j]
                matrix[1, position, m] = filt_high[j]
    return matrix


OFFSETS = ((1, 0), (-1, 0), (0, 1), (0, -1), (1, 1), (1, -1), (-1, 1), (-1, -1))
EXCHANGE_IDS = [0]


def windows(offset, size, halo_len):
    if offset == 1:
        return size - halo_len, halo_len
    if offset == -1:
        return 0, halo_len
    return 0, size


def exchange_kernel(layouts, mesh_x, mesh_y, *refs):
    count = len(OFFSETS)
    arrays = len(layouts)
    sources = refs[:arrays]
    targets = refs[arrays : arrays + arrays * count]
    send_sem, recv_sem = refs[arrays + arrays * count], refs[arrays + arrays * count + 1]
    me_x = lax.axis_index("gx")
    me_y = lax.axis_index("gy")
    peers = [
        (lax.rem(me_x + np.int32(ox + mesh_x), np.int32(mesh_x)), lax.rem(me_y + np.int32(oy + mesh_y), np.int32(mesh_y)))
        for ox, oy in OFFSETS
    ]
    barrier = pltpu.get_barrier_semaphore()
    for peer in peers:
        pl.semaphore_signal(barrier, inc=1, device_id=peer, device_id_type=pl.DeviceIdType.MESH)
    pl.semaphore_wait(barrier, count)
    copies = []
    for n, (ndim, dx, hx, size_x, dy, hy, size_y) in enumerate(layouts):
        for s, ((ox, oy), peer) in enumerate(zip(OFFSETS, peers)):
            index = [slice(None)] * ndim
            index[dx] = pl.ds(*windows(ox, size_x, hx))
            index[dy] = pl.ds(*windows(oy, size_y, hy))
            slot = n * count + s
            copy = pltpu.make_async_remote_copy(
                src_ref=sources[n].at[tuple(index)],
                dst_ref=targets[slot],
                send_sem=send_sem.at[slot],
                recv_sem=recv_sem.at[slot],
                device_id=peer,
                device_id_type=pl.DeviceIdType.MESH,
            )
            copy.start()
            copies.append(copy)
    for copy in copies:
        copy.wait()


def piece_shape(array, dx, hx, dy, hy, offset):
    shape = list(array.shape)
    shape[dx] = windows(offset[0], shape[dx], hx)[1]
    shape[dy] = windows(offset[1], shape[dy], hy)[1]
    return jax.ShapeDtypeStruct(tuple(shape), array.dtype)


def halos(requests):
    cid = EXCHANGE_IDS[0]
    EXCHANGE_IDS[0] += 1
    count = len(OFFSETS)
    layouts = tuple(
        (array.ndim, dx, hx, array.shape[dx], dy, hy, array.shape[dy]) for array, dx, hx, dy, hy in requests
    )
    shapes = [piece_shape(array, dx, hx, dy, hy, offset) for array, dx, hx, dy, hy in requests for offset in OFFSETS]
    received = pl.pallas_call(
        functools.partial(exchange_kernel, layouts, lax.axis_size("gx"), lax.axis_size("gy")),
        out_shape=shapes,
        in_specs=[pl.BlockSpec(memory_space=pl.ANY)] * len(requests),
        out_specs=[pl.BlockSpec(memory_space=pl.ANY)] * len(shapes),
        scratch_shapes=[pltpu.SemaphoreType.DMA((len(shapes),)), pltpu.SemaphoreType.DMA((len(shapes),))],
        compiler_params=pltpu.CompilerParams(collective_id=cid, has_side_effects=True),
    )(*[request[0] for request in requests])
    return [
        assemble(array, dx, dy, received[n * count : (n + 1) * count])
        for n, (array, dx, hx, dy, hy) in enumerate(requests)
    ]


def assemble(array, dx, dy, received):
    before_x, after_x, before_y, after_y, corner_bb, corner_ba, corner_ab, corner_aa = received
    top = jnp.concatenate([corner_bb, before_x, corner_ba], axis=dy)
    mid = jnp.concatenate([before_y, array, after_y], axis=dy)
    bottom = jnp.concatenate([corner_ab, after_x, corner_aa], axis=dy)
    return jnp.concatenate([top, mid, bottom], axis=dx)


def halo(array, dx, hx, dy, hy):
    return halos([(array, dx, hx, dy, hy)])[0]


def contract(left, right, dims, batch):
    return lax.dot_general(
        left, right, (dims, batch), precision=PREC, preferred_element_type=jnp.float32
    )


def batched_left(matrix, data):
    spread = jnp.broadcast_to(jnp.asarray(matrix), (data.shape[0],) + matrix.shape)
    return contract(spread, data, ((1,), (1,)), ((0,), (0,)))


def analyse_lead(extended):
    count = extended.shape[0] - 6
    low = 0.0
    high = 0.0
    for j in range(8):
        taken = lax.slice_in_dim(extended, j, j + count - 1, 2, 0)
        low = low + filt_low[j] * taken
        high = high + filt_high[j] * taken
    return jnp.concatenate([low, high], axis=0)


def synthesise_lead(low_ext, high_ext):
    half = low_ext.shape[0] - 4
    even = 0.0
    odd = 0.0
    for j in range(8):
        if j % 2 == 1:
            start = (3 - j) // 2 + 2
        else:
            start = (4 - j) // 2 + 2
        term = filt_low[j] * low_ext[start : start + half] + filt_high[j] * high_ext[start : start + half]
        if j % 2 == 1:
            even = even + term
        else:
            odd = odd + term
    joined = jnp.stack([even, odd], axis=1)
    return joined.reshape((2 * half,) + even.shape[1:])


def analysis_ext(extended):
    x_part = analyse_lead(extended)
    y_part = batched_left(split_analysis(x_part.shape[1] - 6), x_part)
    size_x, size_y, size_z = y_part.shape
    matrix = jnp.asarray(periodic_analysis(size_z))
    if size_y % 8 == 0:
        flat = contract(y_part.reshape(size_x * size_y, size_z), matrix, ((1,), (0,)), ((), ()))
        return flat.reshape(size_x, size_y, size_z)
    return contract(y_part, matrix, ((2,), (0,)), ((), ()))


def shrink_field(coeffs, thr_table, indices):
    size_x, size_y, size_z = coeffs.shape
    matched = indices[:, None] == jnp.arange(thr_table.shape[0], dtype=jnp.int32)[None, :]
    seven = jnp.sum(jnp.where(matched, thr_table[None, :], 0.0), axis=1)
    eight = jnp.concatenate([jnp.zeros((1,), jnp.float32), seven])
    high_x = (jnp.arange(size_x, dtype=jnp.int32) >= size_x // 2).astype(jnp.int32)
    high_y = (jnp.arange(size_y, dtype=jnp.int32) >= size_y // 2).astype(jnp.int32)
    high_z = (jnp.arange(size_z, dtype=jnp.int32) >= size_z // 2).astype(jnp.int32)
    band_ids = 4 * high_x[:, None, None] + 2 * high_y[None, :, None] + high_z[None, None, :]
    thresh = jnp.zeros(coeffs.shape, jnp.float32)
    for band_no in range(1, 8):
        thresh = jnp.where(band_ids == band_no, eight[band_no], thresh)
    return jnp.sign(coeffs) * jnp.maximum(jnp.abs(coeffs) - thresh, 0.0)


def synthesis_ext(extended):
    two, hx4, _, hy4, size_z = extended.shape
    z_part = contract(extended, jnp.asarray(periodic_analysis(size_z)), ((4,), (1,)), ((), ()))
    z_part = z_part.reshape(2 * hx4, 2, hy4, size_z)
    size_y = 2 * (hy4 - 4)
    matrix = split_synthesis(size_y)
    y_part = batched_left(matrix[0], z_part[:, 0]) + batched_left(matrix[1], z_part[:, 1])
    y_part = y_part.reshape(2, hx4, size_y, size_z)
    return synthesise_lead(y_part[0], y_part[1])


def blocked(cube):
    size_x, size_y, size_z = cube.shape
    return cube.reshape(2, size_x // 2, 2, size_y // 2, size_z)


def low_corner(cube):
    size_x, size_y, size_z = cube.shape
    return cube[: size_x // 2, : size_y // 2, : size_z // 2]


def local(velocity, threshold_table, band_index):
    EXCHANGE_IDS[0] = 0
    cube0 = analysis_ext(halo(velocity, 0, 3, 1, 3))
    shrunk0 = blocked(shrink_field(cube0, threshold_table, band_index[0]))
    ext1, ext0 = halos([(low_corner(cube0), 0, 9, 1, 9), (shrunk0, 1, 2, 3, 2)])
    cube1 = analysis_ext(ext1)
    shrunk1 = blocked(shrink_field(cube1, threshold_table, band_index[1]))
    cube2 = analysis_ext(low_corner(cube1))
    shrunk2 = shrink_field(cube2, threshold_table, band_index[2])
    full2 = lax.dynamic_update_slice(shrunk2, low_corner(cube2), (0, 0, 0))
    recon2 = synthesis_ext(halo(blocked(full2), 1, 4, 3, 4))
    recon2 = recon2[1 : recon2.shape[0] - 1, 1 : recon2.shape[1] - 1]
    half_z = shrunk1.shape[4] // 2
    recon1 = synthesis_ext(shrunk1.at[0, :, 0, :, :half_z].set(recon2))
    half_z = ext0.shape[4] // 2
    return synthesis_ext(ext0.at[0, :, 0, :, :half_z].set(recon1))


def solution(mesh):
    return jax.shard_map(
        local,
        mesh=mesh,
        in_specs=(P("gx", "gy", None), P(), P()),
        out_specs=P("gx", "gy", None),
        check_vma=False,
    )
```

```python
import functools

import jax
import jax.numpy as jnp
import numpy as np
from jax import lax
from jax.experimental import pallas as pl
from jax.experimental.pallas import tpu as pltpu
from jax.sharding import PartitionSpec as P

LEVELS = 3
PREC = lax.Precision.HIGH

filt_low = [
    0.23037781330885523,
    0.7148465705525415,
    0.6308807679295904,
    -0.02798376941698385,
    -0.18703481171888114,
    0.030841381835986965,
    0.032883011666982945,
    -0.010597401784997278,
]
filt_high = [(-1.0) ** j * filt_low[7 - j] for j in range(8)]


def split_analysis(length):
    matrix = np.zeros((length + 6, length), np.float32)
    for k in range(length // 2):
        for j in range(8):
            matrix[2 * k + j, k] = filt_low[j]
            matrix[2 * k + j, length // 2 + k] = filt_high[j]
    return matrix


def periodic_analysis(length):
    matrix = np.zeros((length, length), np.float32)
    for k in range(length // 2):
        for j in range(8):
            matrix[(2 * k + j - 3) % length, k] += filt_low[j]
            matrix[(2 * k + j - 3) % length, length // 2 + k] += filt_high[j]
    return matrix


def split_synthesis(length):
    half_len = length // 2
    matrix = np.zeros((2, half_len + 4, length), np.float32)
    for position in range(half_len + 4):
        k = position - 2
        for m in range(length):
            j = m + 3 - 2 * k
            if 0 <= j < 8:
                matrix[0, position, m] = filt_low[j]
                matrix[1, position, m] = filt_high[j]
    return matrix


OFFSETS = ((1, 0), (-1, 0), (0, 1), (0, -1), (1, 1), (1, -1), (-1, 1), (-1, -1))
EXCHANGE_IDS = [0]


def windows(offset, size, halo_len):
    if offset == 1:
        return size - halo_len, halo_len
    if offset == -1:
        return 0, halo_len
    return 0, size


def exchange_kernel(layouts, mesh_x, mesh_y, *refs):
    count = len(OFFSETS)
    arrays = len(layouts)
    sources = refs[:arrays]
    targets = refs[arrays : arrays + arrays * count]
    send_sem, recv_sem = refs[arrays + arrays * count], refs[arrays + arrays * count + 1]
    me_x = lax.axis_index("gx")
    me_y = lax.axis_index("gy")
    peers = [
        (lax.rem(me_x + np.int32(ox + mesh_x), np.int32(mesh_x)), lax.rem(me_y + np.int32(oy + mesh_y), np.int32(mesh_y)))
        for ox, oy in OFFSETS
    ]
    barrier = pltpu.get_barrier_semaphore()
    for peer in peers:
        pl.semaphore_signal(barrier, inc=1, device_id=peer, device_id_type=pl.DeviceIdType.MESH)
    pl.semaphore_wait(barrier, count)
    copies = []
    for n, (ndim, dx, hx, size_x, dy, hy, size_y) in enumerate(layouts):
        for s, ((ox, oy), peer) in enumerate(zip(OFFSETS, peers)):
            index = [slice(None)] * ndim
            index[dx] = pl.ds(*windows(ox, size_x, hx))
            index[dy] = pl.ds(*windows(oy, size_y, hy))
            slot = n * count + s
            copy = pltpu.make_async_remote_copy(
                src_ref=sources[n].at[tuple(index)],
                dst_ref=targets[slot],
                send_sem=send_sem.at[slot],
                recv_sem=recv_sem.at[slot],
                device_id=peer,
                device_id_type=pl.DeviceIdType.MESH,
            )
            copy.start()
            copies.append(copy)
    for copy in copies:
        copy.wait()


def piece_shape(array, dx, hx, dy, hy, offset):
    shape = list(array.shape)
    shape[dx] = windows(offset[0], shape[dx], hx)[1]
    shape[dy] = windows(offset[1], shape[dy], hy)[1]
    return jax.ShapeDtypeStruct(tuple(shape), array.dtype)


def halos(requests):
    cid = EXCHANGE_IDS[0]
    EXCHANGE_IDS[0] += 1
    count = len(OFFSETS)
    layouts = tuple(
        (array.ndim, dx, hx, array.shape[dx], dy, hy, array.shape[dy]) for array, dx, hx, dy, hy in requests
    )
    shapes = [piece_shape(array, dx, hx, dy, hy, offset) for array, dx, hx, dy, hy in requests for offset in OFFSETS]
    received = pl.pallas_call(
        functools.partial(exchange_kernel, layouts, lax.axis_size("gx"), lax.axis_size("gy")),
        out_shape=shapes,
        in_specs=[pl.BlockSpec(memory_space=pl.ANY)] * len(requests),
        out_specs=[pl.BlockSpec(memory_space=pl.ANY)] * len(shapes),
        scratch_shapes=[pltpu.SemaphoreType.DMA((len(shapes),)), pltpu.SemaphoreType.DMA((len(shapes),))],
        compiler_params=pltpu.CompilerParams(collective_id=cid, has_side_effects=True),
    )(*[request[0] for request in requests])
    return [
        assemble(array, dx, dy, received[n * count : (n + 1) * count])
        for n, (array, dx, hx, dy, hy) in enumerate(requests)
    ]


def assemble(array, dx, dy, received):
    before_x, after_x, before_y, after_y, corner_bb, corner_ba, corner_ab, corner_aa = received
    top = jnp.concatenate([corner_bb, before_x, corner_ba], axis=dy)
    mid = jnp.concatenate([before_y, array, after_y], axis=dy)
    bottom = jnp.concatenate([corner_ab, after_x, corner_aa], axis=dy)
    return jnp.concatenate([top, mid, bottom], axis=dx)


def halo(array, dx, hx, dy, hy):
    return halos([(array, dx, hx, dy, hy)])[0]


def contract(left, right, dims, batch):
    return lax.dot_general(
        left, right, (dims, batch), precision=PREC, preferred_element_type=jnp.float32
    )


def batched_left(matrix, data):
    spread = jnp.broadcast_to(jnp.asarray(matrix), (data.shape[0],) + matrix.shape)
    return contract(spread, data, ((1,), (1,)), ((0,), (0,)))


def analyse_lead(extended):
    count = extended.shape[0] - 6
    low = 0.0
    high = 0.0
    for j in range(8):
        taken = lax.slice_in_dim(extended, j, j + count - 1, 2, 0)
        low = low + filt_low[j] * taken
        high = high + filt_high[j] * taken
    return jnp.concatenate([low, high], axis=0)


def synthesise_lead(low_ext, high_ext):
    half = low_ext.shape[0] - 4
    even = 0.0
    odd = 0.0
    for j in range(8):
        if j % 2 == 1:
            start = (3 - j) // 2 + 2
        else:
            start = (4 - j) // 2 + 2
        term = filt_low[j] * low_ext[start : start + half] + filt_high[j] * high_ext[start : start + half]
        if j % 2 == 1:
            even = even + term
        else:
            odd = odd + term
    joined = jnp.stack([even, odd], axis=1)
    return joined.reshape((2 * half,) + even.shape[1:])


def analysis_ext(extended):
    x_part = analyse_lead(extended)
    y_part = batched_left(split_analysis(x_part.shape[1] - 6), x_part)
    size_x, size_y, size_z = y_part.shape
    matrix = jnp.asarray(periodic_analysis(size_z))
    if size_y % 8 == 0:
        flat = contract(y_part.reshape(size_x * size_y, size_z), matrix, ((1,), (0,)), ((), ()))
        return flat.reshape(size_x, size_y, size_z)
    return contract(y_part, matrix, ((2,), (0,)), ((), ()))


def shrink_field(coeffs, thr_table, indices):
    size_x, size_y, size_z = coeffs.shape
    matched = indices[:, None] == jnp.arange(thr_table.shape[0], dtype=jnp.int32)[None, :]
    seven = jnp.sum(jnp.where(matched, thr_table[None, :], 0.0), axis=1)
    eight = jnp.concatenate([jnp.zeros((1,), jnp.float32), seven])
    high_x = (jnp.arange(size_x, dtype=jnp.int32) >= size_x // 2).astype(jnp.int32)
    high_y = (jnp.arange(size_y, dtype=jnp.int32) >= size_y // 2).astype(jnp.int32)
    plane_ids = 4 * high_x[:, None] + 2 * high_y[None, :]
    low_z = jnp.zeros((size_x, size_y), jnp.float32)
    high_z = jnp.zeros((size_x, size_y), jnp.float32)
    for band_no in range(1, 8):
        if band_no % 2 == 0:
            low_z = jnp.where(plane_ids == band_no, eight[band_no], low_z)
        else:
            high_z = jnp.where(plane_ids + 1 == band_no, eight[band_no], high_z)
    in_high = (jnp.arange(size_z, dtype=jnp.int32) >= size_z // 2)[None, None, :]
    thresh = jnp.where(in_high, high_z[:, :, None], low_z[:, :, None])
    return jnp.sign(coeffs) * jnp.maximum(jnp.abs(coeffs) - thresh, 0.0)


def synthesis_ext(extended, trim=0):
    two, hx4, _, hy4, size_z = extended.shape
    z_part = contract(extended, jnp.asarray(periodic_analysis(size_z)), ((4,), (1,)), ((), ()))
    z_part = z_part.reshape(2 * hx4, 2, hy4, size_z)
    size_y = 2 * (hy4 - 4)
    matrix = split_synthesis(size_y)
    if trim:
        matrix = np.ascontiguousarray(matrix[:, :, trim : size_y - trim])
    y_part = batched_left(matrix[0], z_part[:, 0]) + batched_left(matrix[1], z_part[:, 1])
    y_part = y_part.reshape(2, hx4, matrix.shape[2], size_z)
    return synthesise_lead(y_part[0], y_part[1])


def blocked(cube):
    size_x, size_y, size_z = cube.shape
    return cube.reshape(2, size_x // 2, 2, size_y // 2, size_z)


def low_corner(cube):
    size_x, size_y, size_z = cube.shape
    return cube[: size_x // 2, : size_y // 2, : size_z // 2]


def local(velocity, threshold_table, band_index):
    EXCHANGE_IDS[0] = 0
    cube0 = analysis_ext(halo(velocity, 0, 3, 1, 3))
    shrunk0 = blocked(shrink_field(cube0, threshold_table, band_index[0]))
    ext1, ext0 = halos([(low_corner(cube0), 0, 9, 1, 11), (shrunk0, 1, 2, 3, 2)])
    cube1 = analysis_ext(ext1)
    shrunk1 = blocked(shrink_field(cube1, threshold_table, band_index[1]))
    approx2 = low_corner(cube1)
    cube2 = analysis_ext(approx2[:, 1 : approx2.shape[1] - 1])
    shrunk2 = shrink_field(cube2, threshold_table, band_index[2])
    full2 = lax.dynamic_update_slice(shrunk2, low_corner(cube2), (0, 0, 0))
    recon2 = synthesis_ext(halo(blocked(full2), 1, 4, 3, 4))
    recon2 = recon2[1 : recon2.shape[0] - 1]
    half_z = shrunk1.shape[4] // 2
    recon1 = synthesis_ext(shrunk1.at[0, :, 0, :, :half_z].set(recon2), trim=2)
    half_z = ext0.shape[4] // 2
    return synthesis_ext(ext0.at[0, :, 0, :, :half_z].set(recon1))


def solution(mesh):
    return jax.shard_map(
        local,
        mesh=mesh,
        in_specs=(P("gx", "gy", None), P(), P()),
        out_specs=P("gx", "gy", None),
        check_vma=False,
    )
```

```python
import functools

import jax
import jax.numpy as jnp
import numpy as np
from jax import lax
from jax.experimental import pallas as pl
from jax.experimental.pallas import tpu as pltpu
from jax.sharding import PartitionSpec as P

LEVELS = 3
PREC = lax.Precision.HIGH

filt_low = [
    0.23037781330885523,
    0.7148465705525415,
    0.6308807679295904,
    -0.02798376941698385,
    -0.18703481171888114,
    0.030841381835986965,
    0.032883011666982945,
    -0.010597401784997278,
]
filt_high = [(-1.0) ** j * filt_low[7 - j] for j in range(8)]


def split_analysis(length):
    matrix = np.zeros((length + 6, length), np.float32)
    for k in range(length // 2):
        for j in range(8):
            matrix[2 * k + j, k] = filt_low[j]
            matrix[2 * k + j, length // 2 + k] = filt_high[j]
    return matrix


def periodic_analysis(length):
    matrix = np.zeros((length, length), np.float32)
    for k in range(length // 2):
        for j in range(8):
            matrix[(2 * k + j - 3) % length, k] += filt_low[j]
            matrix[(2 * k + j - 3) % length, length // 2 + k] += filt_high[j]
    return matrix


def split_synthesis(length):
    half_len = length // 2
    matrix = np.zeros((2, half_len + 4, length), np.float32)
    for position in range(half_len + 4):
        k = position - 2
        for m in range(length):
            j = m + 3 - 2 * k
            if 0 <= j < 8:
                matrix[0, position, m] = filt_low[j]
                matrix[1, position, m] = filt_high[j]
    return matrix


OFFSETS = ((1, 0), (-1, 0), (0, 1), (0, -1), (1, 1), (1, -1), (-1, 1), (-1, -1))
EXCHANGE_IDS = [0]


def windows(offset, size, halo_len):
    if offset == 1:
        return size - halo_len, halo_len
    if offset == -1:
        return 0, halo_len
    return 0, size


def exchange_kernel(layouts, mesh_x, mesh_y, *refs):
    count = len(OFFSETS)
    arrays = len(layouts)
    sources = refs[:arrays]
    targets = refs[arrays : arrays + arrays * count]
    send_sem, recv_sem = refs[arrays + arrays * count], refs[arrays + arrays * count + 1]
    me_x = lax.axis_index("gx")
    me_y = lax.axis_index("gy")
    peers = [
        (lax.rem(me_x + np.int32(ox + mesh_x), np.int32(mesh_x)), lax.rem(me_y + np.int32(oy + mesh_y), np.int32(mesh_y)))
        for ox, oy in OFFSETS
    ]
    barrier = pltpu.get_barrier_semaphore()
    for peer in peers:
        pl.semaphore_signal(barrier, inc=1, device_id=peer, device_id_type=pl.DeviceIdType.MESH)
    pl.semaphore_wait(barrier, count)
    copies = []
    for n, (ndim, dx, hx, size_x, dy, hy, size_y) in enumerate(layouts):
        for s, ((ox, oy), peer) in enumerate(zip(OFFSETS, peers)):
            index = [slice(None)] * ndim
            index[dx] = pl.ds(*windows(ox, size_x, hx))
            index[dy] = pl.ds(*windows(oy, size_y, hy))
            slot = n * count + s
            copy = pltpu.make_async_remote_copy(
                src_ref=sources[n].at[tuple(index)],
                dst_ref=targets[slot],
                send_sem=send_sem.at[slot],
                recv_sem=recv_sem.at[slot],
                device_id=peer,
                device_id_type=pl.DeviceIdType.MESH,
            )
            copy.start()
            copies.append(copy)
    for copy in copies:
        copy.wait()


def piece_shape(array, dx, hx, dy, hy, offset):
    shape = list(array.shape)
    shape[dx] = windows(offset[0], shape[dx], hx)[1]
    shape[dy] = windows(offset[1], shape[dy], hy)[1]
    return jax.ShapeDtypeStruct(tuple(shape), array.dtype)


def halos(requests):
    cid = EXCHANGE_IDS[0]
    EXCHANGE_IDS[0] += 1
    count = len(OFFSETS)
    layouts = tuple(
        (array.ndim, dx, hx, array.shape[dx], dy, hy, array.shape[dy]) for array, dx, hx, dy, hy in requests
    )
    shapes = [piece_shape(array, dx, hx, dy, hy, offset) for array, dx, hx, dy, hy in requests for offset in OFFSETS]
    received = pl.pallas_call(
        functools.partial(exchange_kernel, layouts, lax.axis_size("gx"), lax.axis_size("gy")),
        out_shape=shapes,
        in_specs=[pl.BlockSpec(memory_space=pl.ANY)] * len(requests),
        out_specs=[pl.BlockSpec(memory_space=pl.ANY)] * len(shapes),
        scratch_shapes=[pltpu.SemaphoreType.DMA((len(shapes),)), pltpu.SemaphoreType.DMA((len(shapes),))],
        compiler_params=pltpu.CompilerParams(collective_id=cid, has_side_effects=True),
    )(*[request[0] for request in requests])
    return [
        assemble(array, dx, dy, received[n * count : (n + 1) * count])
        for n, (array, dx, hx, dy, hy) in enumerate(requests)
    ]


def assemble(array, dx, dy, received):
    before_x, after_x, before_y, after_y, corner_bb, corner_ba, corner_ab, corner_aa = received
    top = jnp.concatenate([corner_bb, before_x, corner_ba], axis=dy)
    mid = jnp.concatenate([before_y, array, after_y], axis=dy)
    bottom = jnp.concatenate([corner_ab, after_x, corner_aa], axis=dy)
    return jnp.concatenate([top, mid, bottom], axis=dx)


def halo(array, dx, hx, dy, hy):
    return halos([(array, dx, hx, dy, hy)])[0]


def contract(left, right, dims, batch):
    return lax.dot_general(
        left, right, (dims, batch), precision=PREC, preferred_element_type=jnp.float32
    )


def batched_left(matrix, data):
    spread = jnp.broadcast_to(jnp.asarray(matrix), (data.shape[0],) + matrix.shape)
    return contract(spread, data, ((1,), (1,)), ((0,), (0,)))


def analyse_lead(extended):
    count = extended.shape[0] - 6
    low = 0.0
    high = 0.0
    for j in range(8):
        taken = lax.slice_in_dim(extended, j, j + count - 1, 2, 0)
        low = low + filt_low[j] * taken
        high = high + filt_high[j] * taken
    return jnp.concatenate([low, high], axis=0)


def synthesise_lead(low_ext, high_ext):
    half = low_ext.shape[0] - 4
    even = 0.0
    odd = 0.0
    for j in range(8):
        if j % 2 == 1:
            start = (3 - j) // 2 + 2
        else:
            start = (4 - j) // 2 + 2
        term = filt_low[j] * low_ext[start : start + half] + filt_high[j] * high_ext[start : start + half]
        if j % 2 == 1:
            even = even + term
        else:
            odd = odd + term
    joined = jnp.stack([even, odd], axis=1)
    return joined.reshape((2 * half,) + even.shape[1:])


def analysis_ext(extended):
    x_part = analyse_lead(extended)
    y_part = batched_left(split_analysis(x_part.shape[1] - 6), x_part)
    size_x, size_y, size_z = y_part.shape
    matrix = jnp.asarray(periodic_analysis(size_z))
    if size_y % 8 == 0:
        flat = contract(y_part.reshape(size_x * size_y, size_z), matrix, ((1,), (0,)), ((), ()))
        return flat.reshape(size_x, size_y, size_z)
    return contract(y_part, matrix, ((2,), (0,)), ((), ()))


def shrink_field(coeffs, thr_table, indices):
    size_x, size_y, size_z = coeffs.shape
    matched = indices[:, None] == jnp.arange(thr_table.shape[0], dtype=jnp.int32)[None, :]
    seven = jnp.sum(jnp.where(matched, thr_table[None, :], 0.0), axis=1)
    eight = jnp.concatenate([jnp.zeros((1,), jnp.float32), seven])
    high_x = (jnp.arange(size_x, dtype=jnp.int32) >= size_x // 2).astype(jnp.int32)
    high_y = (jnp.arange(size_y, dtype=jnp.int32) >= size_y // 2).astype(jnp.int32)
    plane_ids = 4 * high_x[:, None] + 2 * high_y[None, :]
    low_z = jnp.zeros((size_x, size_y), jnp.float32)
    high_z = jnp.zeros((size_x, size_y), jnp.float32)
    for band_no in range(1, 8):
        if band_no % 2 == 0:
            low_z = jnp.where(plane_ids == band_no, eight[band_no], low_z)
        else:
            high_z = jnp.where(plane_ids + 1 == band_no, eight[band_no], high_z)
    in_high = (jnp.arange(size_z, dtype=jnp.int32) >= size_z // 2)[None, None, :]
    thresh = jnp.where(in_high, high_z[:, :, None], low_z[:, :, None])
    return jnp.sign(coeffs) * jnp.maximum(jnp.abs(coeffs) - thresh, 0.0)


def synthesis_ext(extended, trim=0):
    two, hx4, _, hy4, size_z = extended.shape
    z_part = contract(extended, jnp.asarray(periodic_analysis(size_z)), ((4,), (1,)), ((), ()))
    z_part = z_part.reshape(2 * hx4, 2, hy4, size_z)
    size_y = 2 * (hy4 - 4)
    matrix = split_synthesis(size_y)
    if trim:
        matrix = np.ascontiguousarray(matrix[:, :, trim : size_y - trim])
    y_part = batched_left(matrix[0], z_part[:, 0]) + batched_left(matrix[1], z_part[:, 1])
    y_part = y_part.reshape(2, hx4, matrix.shape[2], size_z)
    return synthesise_lead(y_part[0], y_part[1])


def blocked(cube):
    size_x, size_y, size_z = cube.shape
    return cube.reshape(2, size_x // 2, 2, size_y // 2, size_z)


def low_corner(cube):
    size_x, size_y, size_z = cube.shape
    return cube[: size_x // 2, : size_y // 2, : size_z // 2]


def local(velocity, threshold_table, band_index):
    EXCHANGE_IDS[0] = 0
    cube0 = analysis_ext(halo(velocity, 0, 3, 1, 3))
    shrunk0 = blocked(shrink_field(cube0, threshold_table, band_index[0]))
    ext1, ext0 = halos([(low_corner(cube0), 0, 9, 1, 11), (shrunk0, 1, 2, 3, 2)])
    cube1 = analysis_ext(ext1)
    approx2 = low_corner(cube1)
    cube2 = analysis_ext(approx2[:, 1 : approx2.shape[1] - 1])
    shrunk2 = shrink_field(cube2, threshold_table, band_index[2])
    full2 = lax.dynamic_update_slice(shrunk2, low_corner(cube2), (0, 0, 0))
    recon2 = synthesis_ext(halo(blocked(full2), 1, 4, 3, 4))
    recon2 = recon2[1 : recon2.shape[0] - 1]
    shrunk1 = shrink_field(cube1, threshold_table, band_index[1])
    size1 = cube1.shape
    padded2 = jnp.pad(recon2, [(0, size1[d] - recon2.shape[d]) for d in range(3)])
    in_band0 = (
        (lax.broadcasted_iota(jnp.int32, size1, 0) < size1[0] // 2)
        & (lax.broadcasted_iota(jnp.int32, size1, 1) < size1[1] // 2)
        & (lax.broadcasted_iota(jnp.int32, size1, 2) < size1[2] // 2)
    )
    recon1 = synthesis_ext(blocked(jnp.where(in_band0, padded2, shrunk1)), trim=2)
    half_z = ext0.shape[4] // 2
    return synthesis_ext(ext0.at[0, :, 0, :, :half_z].set(recon1))


def solution(mesh):
    return jax.shard_map(
        local,
        mesh=mesh,
        in_specs=(P("gx", "gy", None), P(), P()),
        out_specs=P("gx", "gy", None),
        check_vma=False,
    )
```

```python
import functools

import jax
import jax.numpy as jnp
import numpy as np
from jax import lax
from jax.experimental import pallas as pl
from jax.experimental.pallas import tpu as pltpu
from jax.sharding import PartitionSpec as P

LEVELS = 3
PREC = lax.Precision.HIGH

filt_low = [
    0.23037781330885523,
    0.7148465705525415,
    0.6308807679295904,
    -0.02798376941698385,
    -0.18703481171888114,
    0.030841381835986965,
    0.032883011666982945,
    -0.010597401784997278,
]
filt_high = [(-1.0) ** j * filt_low[7 - j] for j in range(8)]


def split_analysis(length):
    matrix = np.zeros((length + 6, length), np.float32)
    for k in range(length // 2):
        for j in range(8):
            matrix[2 * k + j, k] = filt_low[j]
            matrix[2 * k + j, length // 2 + k] = filt_high[j]
    return matrix


def periodic_analysis(length):
    matrix = np.zeros((length, length), np.float32)
    for k in range(length // 2):
        for j in range(8):
            matrix[(2 * k + j - 3) % length, k] += filt_low[j]
            matrix[(2 * k + j - 3) % length, length // 2 + k] += filt_high[j]
    return matrix


def split_synthesis(length):
    half_len = length // 2
    matrix = np.zeros((2, half_len + 4, length), np.float32)
    for position in range(half_len + 4):
        k = position - 2
        for m in range(length):
            j = m + 3 - 2 * k
            if 0 <= j < 8:
                matrix[0, position, m] = filt_low[j]
                matrix[1, position, m] = filt_high[j]
    return matrix


OFFSETS = ((1, 0), (-1, 0), (0, 1), (0, -1), (1, 1), (1, -1), (-1, 1), (-1, -1))
EXCHANGE_IDS = [0]


def windows(offset, size, halo_len):
    if offset == 1:
        return size - halo_len, halo_len
    if offset == -1:
        return 0, halo_len
    return 0, size


def exchange_kernel(layouts, mesh_x, mesh_y, *refs):
    count = len(OFFSETS)
    arrays = len(layouts)
    sources = refs[:arrays]
    targets = refs[arrays : arrays + arrays * count]
    send_sem, recv_sem = refs[arrays + arrays * count], refs[arrays + arrays * count + 1]
    me_x = lax.axis_index("gx")
    me_y = lax.axis_index("gy")
    peers = [
        (lax.rem(me_x + np.int32(ox + mesh_x), np.int32(mesh_x)), lax.rem(me_y + np.int32(oy + mesh_y), np.int32(mesh_y)))
        for ox, oy in OFFSETS
    ]
    barrier = pltpu.get_barrier_semaphore()
    for peer in peers:
        pl.semaphore_signal(barrier, inc=1, device_id=peer, device_id_type=pl.DeviceIdType.MESH)
    pl.semaphore_wait(barrier, count)
    copies = []
    for n, (ndim, dx, hx, size_x, dy, hy, size_y) in enumerate(layouts):
        for s, ((ox, oy), peer) in enumerate(zip(OFFSETS, peers)):
            index = [slice(None)] * ndim
            index[dx] = pl.ds(*windows(ox, size_x, hx))
            index[dy] = pl.ds(*windows(oy, size_y, hy))
            slot = n * count + s
            copy = pltpu.make_async_remote_copy(
                src_ref=sources[n].at[tuple(index)],
                dst_ref=targets[slot],
                send_sem=send_sem.at[slot],
                recv_sem=recv_sem.at[slot],
                device_id=peer,
                device_id_type=pl.DeviceIdType.MESH,
            )
            copy.start()
            copies.append(copy)
    for copy in copies:
        copy.wait()


def piece_shape(array, dx, hx, dy, hy, offset):
    shape = list(array.shape)
    shape[dx] = windows(offset[0], shape[dx], hx)[1]
    shape[dy] = windows(offset[1], shape[dy], hy)[1]
    return jax.ShapeDtypeStruct(tuple(shape), array.dtype)


def halos(requests):
    cid = EXCHANGE_IDS[0]
    EXCHANGE_IDS[0] += 1
    count = len(OFFSETS)
    layouts = tuple(
        (array.ndim, dx, hx, array.shape[dx], dy, hy, array.shape[dy]) for array, dx, hx, dy, hy in requests
    )
    shapes = [piece_shape(array, dx, hx, dy, hy, offset) for array, dx, hx, dy, hy in requests for offset in OFFSETS]
    received = pl.pallas_call(
        functools.partial(exchange_kernel, layouts, lax.axis_size("gx"), lax.axis_size("gy")),
        out_shape=shapes,
        in_specs=[pl.BlockSpec(memory_space=pl.ANY)] * len(requests),
        out_specs=[pl.BlockSpec(memory_space=pl.ANY)] * len(shapes),
        scratch_shapes=[pltpu.SemaphoreType.DMA((len(shapes),)), pltpu.SemaphoreType.DMA((len(shapes),))],
        compiler_params=pltpu.CompilerParams(collective_id=cid, has_side_effects=True),
    )(*[request[0] for request in requests])
    return [
        assemble(array, dx, dy, received[n * count : (n + 1) * count])
        for n, (array, dx, hx, dy, hy) in enumerate(requests)
    ]


def assemble(array, dx, dy, received):
    before_x, after_x, before_y, after_y, corner_bb, corner_ba, corner_ab, corner_aa = received
    top = jnp.concatenate([corner_bb, before_x, corner_ba], axis=dy)
    mid = jnp.concatenate([before_y, array, after_y], axis=dy)
    bottom = jnp.concatenate([corner_ab, after_x, corner_aa], axis=dy)
    return jnp.concatenate([top, mid, bottom], axis=dx)


def halo(array, dx, hx, dy, hy):
    return halos([(array, dx, hx, dy, hy)])[0]


def contract(left, right, dims, batch):
    return lax.dot_general(
        left, right, (dims, batch), precision=PREC, preferred_element_type=jnp.float32
    )


def batched_left(matrix, data):
    spread = jnp.broadcast_to(jnp.asarray(matrix), (data.shape[0],) + matrix.shape)
    return contract(spread, data, ((1,), (1,)), ((0,), (0,)))


def analyse_lead(extended):
    count = extended.shape[0] - 6
    low = 0.0
    high = 0.0
    for j in range(8):
        taken = lax.slice_in_dim(extended, j, j + count - 1, 2, 0)
        low = low + filt_low[j] * taken
        high = high + filt_high[j] * taken
    return jnp.concatenate([low, high], axis=0)


def synthesise_lead(low_ext, high_ext):
    half = low_ext.shape[0] - 4
    even = 0.0
    odd = 0.0
    for j in range(8):
        if j % 2 == 1:
            start = (3 - j) // 2 + 2
        else:
            start = (4 - j) // 2 + 2
        term = filt_low[j] * low_ext[start : start + half] + filt_high[j] * high_ext[start : start + half]
        if j % 2 == 1:
            even = even + term
        else:
            odd = odd + term
    joined = jnp.stack([even, odd], axis=1)
    return joined.reshape((2 * half,) + even.shape[1:])


def analysis_ext(extended):
    x_part = analyse_lead(extended)
    y_part = batched_left(split_analysis(x_part.shape[1] - 6), x_part)
    size_x, size_y, size_z = y_part.shape
    matrix = jnp.asarray(periodic_analysis(size_z))
    if size_y % 8 == 0:
        flat = contract(y_part.reshape(size_x * size_y, size_z), matrix, ((1,), (0,)), ((), ()))
        return flat.reshape(size_x, size_y, size_z)
    return contract(y_part, matrix, ((2,), (0,)), ((), ()))


def shrink_field(coeffs, thr_table, indices):
    size_x, size_y, size_z = coeffs.shape
    matched = indices[:, None] == jnp.arange(thr_table.shape[0], dtype=jnp.int32)[None, :]
    seven = jnp.sum(jnp.where(matched, thr_table[None, :], 0.0), axis=1)
    eight = jnp.concatenate([jnp.zeros((1,), jnp.float32), seven])
    high_x = (jnp.arange(size_x, dtype=jnp.int32) >= size_x // 2).astype(jnp.int32)
    high_y = (jnp.arange(size_y, dtype=jnp.int32) >= size_y // 2).astype(jnp.int32)
    plane_ids = 4 * high_x[:, None] + 2 * high_y[None, :]
    low_z = jnp.zeros((size_x, size_y), jnp.float32)
    high_z = jnp.zeros((size_x, size_y), jnp.float32)
    for band_no in range(1, 8):
        if band_no % 2 == 0:
            low_z = jnp.where(plane_ids == band_no, eight[band_no], low_z)
        else:
            high_z = jnp.where(plane_ids + 1 == band_no, eight[band_no], high_z)
    in_high = (jnp.arange(size_z, dtype=jnp.int32) >= size_z // 2)[None, None, :]
    thresh = jnp.where(in_high, high_z[:, :, None], low_z[:, :, None])
    return jnp.sign(coeffs) * jnp.maximum(jnp.abs(coeffs) - thresh, 0.0)


def synthesis_ext(extended, trim=0):
    two, hx4, _, hy4, size_z = extended.shape
    z_part = contract(extended, jnp.asarray(periodic_analysis(size_z)), ((4,), (1,)), ((), ()))
    z_part = z_part.reshape(2 * hx4, 2, hy4, size_z)
    size_y = 2 * (hy4 - 4)
    matrix = split_synthesis(size_y)
    if trim:
        matrix = np.ascontiguousarray(matrix[:, :, trim : size_y - trim])
    y_part = batched_left(matrix[0], z_part[:, 0]) + batched_left(matrix[1], z_part[:, 1])
    y_part = y_part.reshape(2, hx4, matrix.shape[2], size_z)
    return synthesise_lead(y_part[0], y_part[1])


def blocked(cube):
    size_x, size_y, size_z = cube.shape
    return cube.reshape(2, size_x // 2, 2, size_y // 2, size_z)


def low_corner(cube):
    size_x, size_y, size_z = cube.shape
    return cube[: size_x // 2, : size_y // 2, : size_z // 2]


def local(velocity, threshold_table, band_index):
    EXCHANGE_IDS[0] = 0
    cube0 = analysis_ext(halo(velocity, 0, 3, 1, 3))
    shrunk0 = blocked(shrink_field(cube0, threshold_table, band_index[0]))
    ext1, ext0 = halos([(low_corner(cube0), 0, 9, 1, 11), (shrunk0, 1, 2, 3, 2)])
    cube1 = analysis_ext(ext1)
    approx2 = low_corner(cube1)
    cube2 = analysis_ext(approx2[:, 1 : approx2.shape[1] - 1])
    shrunk2 = shrink_field(cube2, threshold_table, band_index[2])
    full2 = lax.dynamic_update_slice(shrunk2, low_corner(cube2), (0, 0, 0))
    recon2 = synthesis_ext(halo(blocked(full2), 1, 4, 3, 4))
    recon2 = recon2[1 : recon2.shape[0] - 1]
    shrunk1 = shrink_field(cube1, threshold_table, band_index[1])
    size1 = cube1.shape
    padded2 = jnp.pad(recon2, [(0, size1[d] - recon2.shape[d]) for d in range(3)])
    in_band0 = (
        (lax.broadcasted_iota(jnp.int32, size1, 0) < size1[0] // 2)
        & (lax.broadcasted_iota(jnp.int32, size1, 1) < size1[1] // 2)
        & (lax.broadcasted_iota(jnp.int32, size1, 2) < size1[2] // 2)
    )
    recon1 = synthesis_ext(blocked(jnp.where(in_band0, padded2, shrunk1)), trim=2)
    size0 = ext0.shape
    padded1 = jnp.pad(recon1[None, :, None], [(0, size0[d] - recon1[None, :, None].shape[d]) for d in range(5)])
    in_band0 = (
        (lax.broadcasted_iota(jnp.int32, size0, 0) == 0)
        & (lax.broadcasted_iota(jnp.int32, size0, 2) == 0)
        & (lax.broadcasted_iota(jnp.int32, size0, 4) < size0[4] // 2)
    )
    return synthesis_ext(jnp.where(in_band0, padded1, ext0))


def solution(mesh):
    return jax.shard_map(
        local,
        mesh=mesh,
        in_specs=(P("gx", "gy", None), P(), P()),
        out_specs=P("gx", "gy", None),
        check_vma=False,
    )
```

```python
import functools

import jax
import jax.numpy as jnp
import numpy as np
from jax import lax
from jax.experimental import pallas as pl
from jax.experimental.pallas import tpu as pltpu
from jax.sharding import PartitionSpec as P

LEVELS = 3
PREC = lax.Precision.HIGH

filt_low = [
    0.23037781330885523,
    0.7148465705525415,
    0.6308807679295904,
    -0.02798376941698385,
    -0.18703481171888114,
    0.030841381835986965,
    0.032883011666982945,
    -0.010597401784997278,
]
filt_high = [(-1.0) ** j * filt_low[7 - j] for j in range(8)]


def split_analysis(length):
    matrix = np.zeros((length + 6, length), np.float32)
    for k in range(length // 2):
        for j in range(8):
            matrix[2 * k + j, k] = filt_low[j]
            matrix[2 * k + j, length // 2 + k] = filt_high[j]
    return matrix


def periodic_analysis(length):
    matrix = np.zeros((length, length), np.float32)
    for k in range(length // 2):
        for j in range(8):
            matrix[(2 * k + j - 3) % length, k] += filt_low[j]
            matrix[(2 * k + j - 3) % length, length // 2 + k] += filt_high[j]
    return matrix


def split_synthesis(length):
    half_len = length // 2
    matrix = np.zeros((2, half_len + 4, length), np.float32)
    for position in range(half_len + 4):
        k = position - 2
        for m in range(length):
            j = m + 3 - 2 * k
            if 0 <= j < 8:
                matrix[0, position, m] = filt_low[j]
                matrix[1, position, m] = filt_high[j]
    return matrix


OFFSETS = ((1, 0), (-1, 0), (0, 1), (0, -1), (1, 1), (1, -1), (-1, 1), (-1, -1))
EXCHANGE_IDS = [0]


def windows(offset, size, halo_len):
    if offset == 1:
        return size - halo_len, halo_len
    if offset == -1:
        return 0, halo_len
    return 0, size


def exchange_kernel(layouts, mesh_x, mesh_y, *refs):
    count = len(OFFSETS)
    arrays = len(layouts)
    sources = refs[:arrays]
    targets = refs[arrays : arrays + arrays * count]
    send_sem, recv_sem = refs[arrays + arrays * count], refs[arrays + arrays * count + 1]
    me_x = lax.axis_index("gx")
    me_y = lax.axis_index("gy")
    peers = [
        (lax.rem(me_x + np.int32(ox + mesh_x), np.int32(mesh_x)), lax.rem(me_y + np.int32(oy + mesh_y), np.int32(mesh_y)))
        for ox, oy in OFFSETS
    ]
    barrier = pltpu.get_barrier_semaphore()
    for peer in peers:
        pl.semaphore_signal(barrier, inc=1, device_id=peer, device_id_type=pl.DeviceIdType.MESH)
    pl.semaphore_wait(barrier, count)
    copies = []
    for n, (ndim, dx, hx, size_x, dy, hy, size_y) in enumerate(layouts):
        for s, ((ox, oy), peer) in enumerate(zip(OFFSETS, peers)):
            index = [slice(None)] * ndim
            index[dx] = pl.ds(*windows(ox, size_x, hx))
            index[dy] = pl.ds(*windows(oy, size_y, hy))
            slot = n * count + s
            copy = pltpu.make_async_remote_copy(
                src_ref=sources[n].at[tuple(index)],
                dst_ref=targets[slot],
                send_sem=send_sem.at[slot],
                recv_sem=recv_sem.at[slot],
                device_id=peer,
                device_id_type=pl.DeviceIdType.MESH,
            )
            copy.start()
            copies.append(copy)
    for copy in copies:
        copy.wait()


def piece_shape(array, dx, hx, dy, hy, offset):
    shape = list(array.shape)
    shape[dx] = windows(offset[0], shape[dx], hx)[1]
    shape[dy] = windows(offset[1], shape[dy], hy)[1]
    return jax.ShapeDtypeStruct(tuple(shape), array.dtype)


def halos(requests):
    cid = EXCHANGE_IDS[0]
    EXCHANGE_IDS[0] += 1
    count = len(OFFSETS)
    layouts = tuple(
        (array.ndim, dx, hx, array.shape[dx], dy, hy, array.shape[dy]) for array, dx, hx, dy, hy in requests
    )
    shapes = [piece_shape(array, dx, hx, dy, hy, offset) for array, dx, hx, dy, hy in requests for offset in OFFSETS]
    received = pl.pallas_call(
        functools.partial(exchange_kernel, layouts, lax.axis_size("gx"), lax.axis_size("gy")),
        out_shape=shapes,
        in_specs=[pl.BlockSpec(memory_space=pl.ANY)] * len(requests),
        out_specs=[pl.BlockSpec(memory_space=pl.ANY)] * len(shapes),
        scratch_shapes=[pltpu.SemaphoreType.DMA((len(shapes),)), pltpu.SemaphoreType.DMA((len(shapes),))],
        compiler_params=pltpu.CompilerParams(collective_id=cid, has_side_effects=True),
    )(*[request[0] for request in requests])
    return [
        assemble(array, dx, dy, received[n * count : (n + 1) * count])
        for n, (array, dx, hx, dy, hy) in enumerate(requests)
    ]


def assemble(array, dx, dy, received):
    before_x, after_x, before_y, after_y, corner_bb, corner_ba, corner_ab, corner_aa = received
    top = jnp.concatenate([corner_bb, before_x, corner_ba], axis=dy)
    mid = jnp.concatenate([before_y, array, after_y], axis=dy)
    bottom = jnp.concatenate([corner_ab, after_x, corner_aa], axis=dy)
    return jnp.concatenate([top, mid, bottom], axis=dx)


def halo(array, dx, hx, dy, hy):
    return halos([(array, dx, hx, dy, hy)])[0]


def contract(left, right, dims, batch):
    return lax.dot_general(
        left, right, (dims, batch), precision=PREC, preferred_element_type=jnp.float32
    )


def batched_left(matrix, data):
    spread = jnp.broadcast_to(jnp.asarray(matrix), (data.shape[0],) + matrix.shape)
    return contract(spread, data, ((1,), (1,)), ((0,), (0,)))


def analyse_lead(extended):
    count = extended.shape[0] - 6
    low = 0.0
    high = 0.0
    for j in range(8):
        taken = lax.slice_in_dim(extended, j, j + count - 1, 2, 0)
        low = low + filt_low[j] * taken
        high = high + filt_high[j] * taken
    return jnp.concatenate([low, high], axis=0)


def synthesise_lead(low_ext, high_ext):
    half = low_ext.shape[0] - 4
    even = 0.0
    odd = 0.0
    for j in range(8):
        if j % 2 == 1:
            start = (3 - j) // 2 + 2
        else:
            start = (4 - j) // 2 + 2
        term = filt_low[j] * low_ext[start : start + half] + filt_high[j] * high_ext[start : start + half]
        if j % 2 == 1:
            even = even + term
        else:
            odd = odd + term
    joined = jnp.stack([even, odd], axis=1)
    return joined.reshape((2 * half,) + even.shape[1:])


def analysis_ext(extended):
    x_part = analyse_lead(extended)
    y_part = batched_left(split_analysis(x_part.shape[1] - 6), x_part)
    size_x, size_y, size_z = y_part.shape
    matrix = jnp.asarray(periodic_analysis(size_z))
    if size_y % 8 == 0:
        flat = contract(y_part.reshape(size_x * size_y, size_z), matrix, ((1,), (0,)), ((), ()))
        return flat.reshape(size_x, size_y, size_z)
    return contract(y_part, matrix, ((2,), (0,)), ((), ()))


def shrink_field(coeffs, thr_table, indices):
    size_x, size_y, size_z = coeffs.shape
    matched = indices[:, None] == jnp.arange(thr_table.shape[0], dtype=jnp.int32)[None, :]
    seven = jnp.sum(jnp.where(matched, thr_table[None, :], 0.0), axis=1)
    eight = jnp.concatenate([jnp.zeros((1,), jnp.float32), seven])
    high_x = (jnp.arange(size_x, dtype=jnp.int32) >= size_x // 2).astype(jnp.int32)
    high_y = (jnp.arange(size_y, dtype=jnp.int32) >= size_y // 2).astype(jnp.int32)
    plane_ids = 4 * high_x[:, None] + 2 * high_y[None, :]
    low_z = jnp.zeros((size_x, size_y), jnp.float32)
    high_z = jnp.zeros((size_x, size_y), jnp.float32)
    for band_no in range(1, 8):
        if band_no % 2 == 0:
            low_z = jnp.where(plane_ids == band_no, eight[band_no], low_z)
        else:
            high_z = jnp.where(plane_ids + 1 == band_no, eight[band_no], high_z)
    in_high = (jnp.arange(size_z, dtype=jnp.int32) >= size_z // 2)[None, None, :]
    thresh = jnp.where(in_high, high_z[:, :, None], low_z[:, :, None])
    return jnp.sign(coeffs) * jnp.maximum(jnp.abs(coeffs) - thresh, 0.0)


def synthesis_ext(extended, trim=0):
    two, hx4, _, hy4, size_z = extended.shape
    matrix_z = jnp.asarray(periodic_analysis(size_z))
    if hy4 % 8 == 0:
        flat = extended.reshape(4 * hx4 * hy4, size_z)
        z_part = contract(flat, matrix_z, ((1,), (1,)), ((), ()))
    else:
        z_part = contract(extended, matrix_z, ((4,), (1,)), ((), ()))
    z_part = z_part.reshape(2 * hx4, 2, hy4, size_z)
    size_y = 2 * (hy4 - 4)
    matrix = split_synthesis(size_y)
    if trim:
        matrix = np.ascontiguousarray(matrix[:, :, trim : size_y - trim])
    y_part = batched_left(matrix[0], z_part[:, 0]) + batched_left(matrix[1], z_part[:, 1])
    y_part = y_part.reshape(2, hx4, matrix.shape[2], size_z)
    return synthesise_lead(y_part[0], y_part[1])


def blocked(cube):
    size_x, size_y, size_z = cube.shape
    return cube.reshape(2, size_x // 2, 2, size_y // 2, size_z)


def low_corner(cube):
    size_x, size_y, size_z = cube.shape
    return cube[: size_x // 2, : size_y // 2, : size_z // 2]


def local(velocity, threshold_table, band_index):
    EXCHANGE_IDS[0] = 0
    cube0 = analysis_ext(halo(velocity, 0, 3, 1, 3))
    shrunk0 = blocked(shrink_field(cube0, threshold_table, band_index[0]))
    ext1, ext0 = halos([(low_corner(cube0), 0, 9, 1, 11), (shrunk0, 1, 2, 3, 2)])
    cube1 = analysis_ext(ext1)
    approx2 = low_corner(cube1)
    cube2 = analysis_ext(approx2[:, 1 : approx2.shape[1] - 1])
    shrunk2 = shrink_field(cube2, threshold_table, band_index[2])
    full2 = lax.dynamic_update_slice(shrunk2, low_corner(cube2), (0, 0, 0))
    recon2 = synthesis_ext(halo(blocked(full2), 1, 4, 3, 4))
    recon2 = recon2[1 : recon2.shape[0] - 1]
    shrunk1 = shrink_field(cube1, threshold_table, band_index[1])
    size1 = cube1.shape
    padded2 = jnp.pad(recon2, [(0, size1[d] - recon2.shape[d]) for d in range(3)])
    in_band0 = (
        (lax.broadcasted_iota(jnp.int32, size1, 0) < size1[0] // 2)
        & (lax.broadcasted_iota(jnp.int32, size1, 1) < size1[1] // 2)
        & (lax.broadcasted_iota(jnp.int32, size1, 2) < size1[2] // 2)
    )
    recon1 = synthesis_ext(blocked(jnp.where(in_band0, padded2, shrunk1)), trim=2)
    half_z = ext0.shape[4] // 2
    return synthesis_ext(ext0.at[0, :, 0, :, :half_z].set(recon1))


def solution(mesh):
    return jax.shard_map(
        local,
        mesh=mesh,
        in_specs=(P("gx", "gy", None), P(), P()),
        out_specs=P("gx", "gy", None),
        check_vma=False,
    )
```

```python
import functools

import jax
import jax.numpy as jnp
import numpy as np
from jax import lax
from jax.experimental import pallas as pl
from jax.experimental.pallas import tpu as pltpu
from jax.sharding import PartitionSpec as P

LEVELS = 3
PREC = lax.Precision.HIGH

filt_low = [
    0.23037781330885523,
    0.7148465705525415,
    0.6308807679295904,
    -0.02798376941698385,
    -0.18703481171888114,
    0.030841381835986965,
    0.032883011666982945,
    -0.010597401784997278,
]
filt_high = [(-1.0) ** j * filt_low[7 - j] for j in range(8)]


def split_analysis(length):
    matrix = np.zeros((length + 6, length), np.float32)
    for k in range(length // 2):
        for j in range(8):
            matrix[2 * k + j, k] = filt_low[j]
            matrix[2 * k + j, length // 2 + k] = filt_high[j]
    return matrix


def periodic_analysis(length):
    matrix = np.zeros((length, length), np.float32)
    for k in range(length // 2):
        for j in range(8):
            matrix[(2 * k + j - 3) % length, k] += filt_low[j]
            matrix[(2 * k + j - 3) % length, length // 2 + k] += filt_high[j]
    return matrix


def split_synthesis(length):
    half_len = length // 2
    matrix = np.zeros((2, half_len + 4, length), np.float32)
    for position in range(half_len + 4):
        k = position - 2
        for m in range(length):
            j = m + 3 - 2 * k
            if 0 <= j < 8:
                matrix[0, position, m] = filt_low[j]
                matrix[1, position, m] = filt_high[j]
    return matrix


OFFSETS = ((1, 0), (-1, 0), (0, 1), (0, -1), (1, 1), (1, -1), (-1, 1), (-1, -1))
EXCHANGE_IDS = [0]


def windows(offset, size, halo_len):
    if offset == 1:
        return size - halo_len, halo_len
    if offset == -1:
        return 0, halo_len
    return 0, size


def exchange_kernel(layouts, mesh_x, mesh_y, *refs):
    count = len(OFFSETS)
    arrays = len(layouts)
    sources = refs[:arrays]
    targets = refs[arrays : arrays + arrays * count]
    send_sem, recv_sem = refs[arrays + arrays * count], refs[arrays + arrays * count + 1]
    me_x = lax.axis_index("gx")
    me_y = lax.axis_index("gy")
    peers = [
        (lax.rem(me_x + np.int32(ox + mesh_x), np.int32(mesh_x)), lax.rem(me_y + np.int32(oy + mesh_y), np.int32(mesh_y)))
        for ox, oy in OFFSETS
    ]
    barrier = pltpu.get_barrier_semaphore()
    for peer in peers:
        pl.semaphore_signal(barrier, inc=1, device_id=peer, device_id_type=pl.DeviceIdType.MESH)
    pl.semaphore_wait(barrier, count)
    copies = []
    for n, (ndim, dx, hx, size_x, dy, hy, size_y) in enumerate(layouts):
        for s, ((ox, oy), peer) in enumerate(zip(OFFSETS, peers)):
            index = [slice(None)] * ndim
            index[dx] = pl.ds(*windows(ox, size_x, hx))
            index[dy] = pl.ds(*windows(oy, size_y, hy))
            slot = n * count + s
            copy = pltpu.make_async_remote_copy(
                src_ref=sources[n].at[tuple(index)],
                dst_ref=targets[slot],
                send_sem=send_sem.at[slot],
                recv_sem=recv_sem.at[slot],
                device_id=peer,
                device_id_type=pl.DeviceIdType.MESH,
            )
            copy.start()
            copies.append(copy)
    for copy in copies:
        copy.wait()


def piece_shape(array, dx, hx, dy, hy, offset):
    shape = list(array.shape)
    shape[dx] = windows(offset[0], shape[dx], hx)[1]
    shape[dy] = windows(offset[1], shape[dy], hy)[1]
    return jax.ShapeDtypeStruct(tuple(shape), array.dtype)


def halos(requests):
    cid = EXCHANGE_IDS[0]
    EXCHANGE_IDS[0] += 1
    count = len(OFFSETS)
    layouts = tuple(
        (array.ndim, dx, hx, array.shape[dx], dy, hy, array.shape[dy]) for array, dx, hx, dy, hy in requests
    )
    shapes = [piece_shape(array, dx, hx, dy, hy, offset) for array, dx, hx, dy, hy in requests for offset in OFFSETS]
    received = pl.pallas_call(
        functools.partial(exchange_kernel, layouts, lax.axis_size("gx"), lax.axis_size("gy")),
        out_shape=shapes,
        in_specs=[pl.BlockSpec(memory_space=pl.ANY)] * len(requests),
        out_specs=[pl.BlockSpec(memory_space=pl.ANY)] * len(shapes),
        scratch_shapes=[pltpu.SemaphoreType.DMA((len(shapes),)), pltpu.SemaphoreType.DMA((len(shapes),))],
        compiler_params=pltpu.CompilerParams(collective_id=cid, has_side_effects=True),
    )(*[request[0] for request in requests])
    return [
        assemble(array, dx, dy, received[n * count : (n + 1) * count])
        for n, (array, dx, hx, dy, hy) in enumerate(requests)
    ]


def assemble(array, dx, dy, received):
    before_x, after_x, before_y, after_y, corner_bb, corner_ba, corner_ab, corner_aa = received
    top = jnp.concatenate([corner_bb, before_x, corner_ba], axis=dy)
    mid = jnp.concatenate([before_y, array, after_y], axis=dy)
    bottom = jnp.concatenate([corner_ab, after_x, corner_aa], axis=dy)
    return jnp.concatenate([top, mid, bottom], axis=dx)


def halo(array, dx, hx, dy, hy):
    return halos([(array, dx, hx, dy, hy)])[0]


def contract(left, right, dims, batch):
    return lax.dot_general(
        left, right, (dims, batch), precision=PREC, preferred_element_type=jnp.float32
    )


def batched_left(matrix, data):
    spread = jnp.broadcast_to(jnp.asarray(matrix), (data.shape[0],) + matrix.shape)
    return contract(spread, data, ((1,), (1,)), ((0,), (0,)))


def analyse_lead(extended):
    count = extended.shape[0] - 6
    low = 0.0
    high = 0.0
    for j in range(8):
        taken = lax.slice_in_dim(extended, j, j + count - 1, 2, 0)
        low = low + filt_low[j] * taken
        high = high + filt_high[j] * taken
    return jnp.concatenate([low, high], axis=0)


def synthesise_lead(low_ext, high_ext):
    half = low_ext.shape[0] - 4
    even = 0.0
    odd = 0.0
    for j in range(8):
        if j % 2 == 1:
            start = (3 - j) // 2 + 2
        else:
            start = (4 - j) // 2 + 2
        term = filt_low[j] * low_ext[start : start + half] + filt_high[j] * high_ext[start : start + half]
        if j % 2 == 1:
            even = even + term
        else:
            odd = odd + term
    joined = jnp.stack([even, odd], axis=1)
    return joined.reshape((2 * half,) + even.shape[1:])


def analysis_ext(extended):
    x_part = analyse_lead(extended)
    y_part = batched_left(split_analysis(x_part.shape[1] - 6), x_part)
    size_x, size_y, size_z = y_part.shape
    matrix = jnp.asarray(periodic_analysis(size_z))
    if size_y % 8 == 0:
        flat = contract(y_part.reshape(size_x * size_y, size_z), matrix, ((1,), (0,)), ((), ()))
        return flat.reshape(size_x, size_y, size_z)
    return contract(y_part, matrix, ((2,), (0,)), ((), ()))


def shrink_field(coeffs, thr_table, indices):
    size_x, size_y, size_z = coeffs.shape
    matched = indices[:, None] == jnp.arange(thr_table.shape[0], dtype=jnp.int32)[None, :]
    seven = jnp.sum(jnp.where(matched, thr_table[None, :], 0.0), axis=1)
    eight = jnp.concatenate([jnp.zeros((1,), jnp.float32), seven])
    high_x = (jnp.arange(size_x, dtype=jnp.int32) >= size_x // 2).astype(jnp.int32)
    high_y = (jnp.arange(size_y, dtype=jnp.int32) >= size_y // 2).astype(jnp.int32)
    plane_ids = 4 * high_x[:, None] + 2 * high_y[None, :]
    low_z = jnp.zeros((size_x, size_y), jnp.float32)
    high_z = jnp.zeros((size_x, size_y), jnp.float32)
    for band_no in range(1, 8):
        if band_no % 2 == 0:
            low_z = jnp.where(plane_ids == band_no, eight[band_no], low_z)
        else:
            high_z = jnp.where(plane_ids + 1 == band_no, eight[band_no], high_z)
    in_high = (jnp.arange(size_z, dtype=jnp.int32) >= size_z // 2)[None, None, :]
    thresh = jnp.where(in_high, high_z[:, :, None], low_z[:, :, None])
    return jnp.sign(coeffs) * jnp.maximum(jnp.abs(coeffs) - thresh, 0.0)


def synthesis_ext(extended, trim=0):
    two, hx4, _, hy4, size_z = extended.shape
    matrix_z = jnp.asarray(periodic_analysis(size_z))
    if hy4 % 8 == 0:
        flat = extended.reshape(4 * hx4 * hy4, size_z)
        z_part = contract(flat, matrix_z, ((1,), (1,)), ((), ()))
    else:
        z_part = contract(extended, matrix_z, ((4,), (1,)), ((), ()))
    z_part = z_part.reshape(2 * hx4, 2, hy4, size_z)
    size_y = 2 * (hy4 - 4)
    matrix = split_synthesis(size_y)
    if trim:
        matrix = np.ascontiguousarray(matrix[:, :, trim : size_y - trim])
    y_part = batched_left(matrix[0], z_part[:, 0]) + batched_left(matrix[1], z_part[:, 1])
    y_part = y_part.reshape(2, hx4, matrix.shape[2], size_z)
    return synthesise_lead(y_part[0], y_part[1])


def blocked(cube):
    size_x, size_y, size_z = cube.shape
    return cube.reshape(2, size_x // 2, 2, size_y // 2, size_z)


def low_corner(cube):
    size_x, size_y, size_z = cube.shape
    return cube[: size_x // 2, : size_y // 2, : size_z // 2]


def local(velocity, threshold_table, band_index):
    EXCHANGE_IDS[0] = 0
    cube0 = analysis_ext(halo(velocity, 0, 3, 1, 3))
    shrunk0 = blocked(shrink_field(cube0, threshold_table, band_index[0]))
    ext1, ext0 = halos([(low_corner(cube0), 0, 9, 1, 11), (shrunk0, 1, 2, 3, 4)])
    cube1 = analysis_ext(ext1)
    approx2 = low_corner(cube1)
    cube2 = analysis_ext(approx2[:, 1 : approx2.shape[1] - 1])
    shrunk2 = shrink_field(cube2, threshold_table, band_index[2])
    full2 = lax.dynamic_update_slice(shrunk2, low_corner(cube2), (0, 0, 0))
    recon2 = synthesis_ext(halo(blocked(full2), 1, 4, 3, 4))
    recon2 = recon2[1 : recon2.shape[0] - 1]
    shrunk1 = shrink_field(cube1, threshold_table, band_index[1])
    size1 = cube1.shape
    padded2 = jnp.pad(recon2, [(0, size1[d] - recon2.shape[d]) for d in range(3)])
    in_band0 = (
        (lax.broadcasted_iota(jnp.int32, size1, 0) < size1[0] // 2)
        & (lax.broadcasted_iota(jnp.int32, size1, 1) < size1[1] // 2)
        & (lax.broadcasted_iota(jnp.int32, size1, 2) < size1[2] // 2)
    )
    recon1 = synthesis_ext(blocked(jnp.where(in_band0, padded2, shrunk1)))
    half_z = ext0.shape[4] // 2
    return synthesis_ext(ext0.at[0, :, 0, :, :half_z].set(recon1), trim=4)


def solution(mesh):
    return jax.shard_map(
        local,
        mesh=mesh,
        in_specs=(P("gx", "gy", None), P(), P()),
        out_specs=P("gx", "gy", None),
        check_vma=False,
    )
```
